32 devices in a mesh: fsdp: 16 (over z, y, x), dp: 2 (over core).
Axes of the slice: x: 2, y: 2, z: 4, core: 2. Of those that a mesh axis runs over, the one named last changes fastest.
Arguments:
- tokens: bfloat16 [64, 384, 768], P(('fsdp', 'dp')), may hold values from -6 to 6
- segments: int32 [64, 384], P(('fsdp', 'dp')), may hold values from 0 to 4, never falling along the last dimension, each value on 1 to 360 neighbouring positions
- first_gain: bfloat16 [768], P('fsdp'), may hold values from 0.5 to 1.5
- first_shift: bfloat16 [768], P('fsdp'), may hold values from -1 to 1
- qkv_weight: bfloat16 [768, 2304], P('fsdp'), may hold values from -0.21875 to 0.21875
- query_bias: bfloat16 [768], P('fsdp'), may hold values from -1 to 1
- value_bias: bfloat16 [768], P('fsdp'), may hold values from -1 to 1
- out_weight: bfloat16 [768, 768], P('fsdp'), may hold values from -0.875 to 0.875
- out_bias: bfloat16 [768], P('fsdp'), may hold values from -1 to 1
- second_gain: bfloat16 [768], P('fsdp'), may hold values from 0.5 to 1.5
- second_shift: bfloat16 [768], P('fsdp'), may hold values from -1 to 1
- up_weight: bfloat16 [768, 3072], P('fsdp'), may hold values from -0.21875 to 0.21875
- up_bias: bfloat16 [3072], P('fsdp'), may hold values from -1 to 1
- down_weight: bfloat16 [3072, 768], P('fsdp'), may hold values from -0.109375 to 0.109375
- down_bias: bfloat16 [768], P('fsdp'), may hold values from -1 to 1
- cotangent: bfloat16 [64, 384, 768], P(('fsdp', 'dp')), may hold values from -6 to 6
Outputs:
- layer_out: bfloat16 [64, 384, 768], P(('fsdp', 'dp'))
- tokens_grad: float32 [64, 384, 768], P(('fsdp', 'dp'))
- first_gain_grad: float32 [768], P(('fsdp', 'dp'))
- first_shift_grad: float32 [768], P(('fsdp', 'dp'))
- qkv_weight_grad: float32 [768, 2304], P(('fsdp', 'dp'))
- query_bias_grad: float32 [768], P(('fsdp', 'dp'))
- value_bias_grad: float32 [768], P(('fsdp', 'dp'))
- out_weight_grad: float32 [768, 768], P(('fsdp', 'dp'))
- out_bias_grad: float32 [768], P(('fsdp', 'dp'))
- second_gain_grad: float32 [768], P(('fsdp', 'dp'))
- second_shift_grad: float32 [768], P(('fsdp', 'dp'))
- up_weight_grad: float32 [768, 3072], P(('fsdp', 'dp'))
- up_bias_grad: float32 [3072], P(('fsdp', 'dp'))
- down_weight_grad: float32 [3072, 768], P(('fsdp', 'dp'))
- down_bias_grad: float32 [768], P(('fsdp', 'dp'))
The draws below stay inside these ranges and needn't reach their ends.
Inputs may be any that keep to these rules, and one draw needn't show every extreme that they name: `segments`: segment numbers never fall along a sequence; an image holds 1 to 360 patches.
All inputs are finite; a program needn't handle non-finite values.
Results may differ from the reference program's by a relative error of at most 0.015.
Values may be sent and summed in bfloat16 or wider, within the bound.
A program may use at most 192 MiB of HBM per device.

```python
import math
import jax
import jax.numpy as jnp
import numpy as np
from jax import lax

D = 768
HEADS = 12
HDIM = 64
FF = 3072
SEQ = 384
LONGEST = 360
IMGS = 5
SEQS = 64


def raised(array, key, source, target, parts, factor):
    def block_of(dim):
        return (jnp.arange(array.shape[dim]) // (array.shape[dim] // parts)).reshape((-1,) + (1,) * (array.ndim - 1 - dim))

    first = jax.random.permutation(key, parts)[block_of(target)]
    other_side = (block_of(target) + parts // 2) % parts
    return jnp.where((block_of(source) == first) | (block_of(source) == other_side), factor * array, array)


def levels(stream_key, extent, shards, low, top_value):
    loudness, own = 1.0, jax.random.fold_in(stream_key, 6)
    for dim, shards_of in shards:
        draws = jnp.exp(jax.random.uniform(jax.random.fold_in(own, dim), (shards_of,), jnp.float32, low / len(shards), top_value / len(shards)))
        loudness = loudness * jnp.repeat(draws, extent[dim] // shards_of).reshape([-1 if axis == dim else 1 for axis in range(len(extent))])
    return loudness


def length_profile(number_of, total, bound, lean):
    portions = [(1 << 20) // math.isqrt(standing ** lean) + 1 for standing in range(2, number_of + 1)]
    spare, holding = total - bound - (number_of - 1), [1] * (number_of - 1)
    while spare > 0:
        free = [i for i in range(number_of - 1) if holding[i] < bound]
        whole, left = sum([portions[i] for i in free]), spare
        for i in free:
            addition = min(bound - holding[i], max(1, left * portions[i] // whole), spare)
            holding[i] = holding[i] + addition
            spare = spare - addition
    return np.array([bound] + holding)


def uneven_parts(own_key, count, total, reach, lean):
    if count == 2:
        one = jax.random.randint(own_key, (), max(1, total - reach), min(reach, total - 1) + 1)
        return jnp.stack([one, total - one])
    sizes = jnp.asarray(length_profile(count, total, reach, lean), jnp.int32)
    twos = (count - 1) // 2
    source_of, receiver = sizes[1:1 + 2 * twos:2], sizes[2:2 + 2 * twos:2]
    room = jnp.minimum(source_of - 1, reach - receiver)
    passed = jax.random.randint(jax.random.fold_in(own_key, 1), (twos,), 0, 1 << 20) % (room + 1)
    sizes = sizes.at[1:1 + 2 * twos:2].set(source_of - passed).at[2:2 + 2 * twos:2].set(receiver + passed)
    return sizes[jax.random.permutation(jax.random.fold_in(own_key, 2), count)]


def noise(own_key, dims, width, limit, shards=(), held_as=jnp.bfloat16):
    entries = width * jax.random.normal(own_key, dims, jnp.float32)
    if shards:
        entries = entries * levels(own_key, dims, shards, -0.22, 0.18)
    return jnp.clip(entries, -limit, limit).astype(held_as)


def bell_draw_with(rng, dims, deviation, bound, shards, heavy, held_as=jnp.bfloat16):
    values = deviation * jax.random.normal(rng, dims, jnp.float32)
    if shards:
        values = values * levels(rng, dims, shards, -0.22, 0.18)
    return jnp.clip(raised(values, jax.random.fold_in(rng, 3), *heavy), -bound, bound).astype(held_as)


def setup_inputs(seed: int = 0) -> dict:
    streams_of = jax.random.split(jax.random.key(seed), 17)
    tokens = noise(streams_of[0], (SEQS, SEQ, D), 1.0, 6.0, ((0, 32),))
    segments = jax.vmap(lambda own: jnp.searchsorted(jnp.cumsum(uneven_parts(own, IMGS, SEQ, LONGEST, 2)), jnp.arange(SEQ), side="right"))(jax.random.split(streams_of[1], SEQS)).reshape((SEQS, SEQ)).astype(jnp.int32)
    first_gain = jnp.clip(1.0 + 0.1 * jax.random.normal(streams_of[2], (D,), jnp.float32), 0.5, 1.5).astype(jnp.bfloat16)
    first_shift = noise(streams_of[3], (D,), 0.2, 1.0, ((0, 16),))
    qkv_weight = noise(streams_of[4], (D, 3 * D), D ** -0.5, 0.21875, ((0, 16),))
    query_bias = noise(streams_of[5], (D,), 0.2, 1.0, ((0, 16),))
    value_bias = noise(streams_of[6], (D,), 0.2, 1.0, ((0, 16),))
    out_weight = noise(streams_of[7], (D, D), (D // 16) ** -0.5, 0.875, ((0, 16),))
    out_bias = noise(streams_of[8], (D,), 0.2, 1.0, ((0, 16),))
    second_gain = jnp.clip(1.0 + 0.1 * jax.random.normal(streams_of[9], (D,), jnp.float32), 0.5, 1.5).astype(jnp.bfloat16)
    second_shift = noise(streams_of[10], (D,), 0.2, 1.0, ((0, 16),))
    up_weight = noise(streams_of[11], (D, FF), D ** -0.5, 0.21875, ((0, 16),))
    up_bias = noise(streams_of[12], (FF,), 0.2, 1.0, ((0, 16),))
    down_weight = noise(streams_of[13], (FF, D), FF ** -0.5, 0.109375, ((0, 16),))
    down_bias = noise(streams_of[14], (D,), 0.2, 1.0, ((0, 16),))
    cotangent = bell_draw_with(streams_of[15], (SEQS, SEQ, D), 1.0, 6.0, ((0, 32),), (0, 2, 32, 2.75))
    return {"tokens": tokens, "segments": segments, "first_gain": first_gain, "first_shift": first_shift, "qkv_weight": qkv_weight, "query_bias": query_bias, "value_bias": value_bias, "out_weight": out_weight, "out_bias": out_bias, "second_gain": second_gain, "second_shift": second_shift, "up_weight": up_weight, "up_bias": up_bias, "down_weight": down_weight, "down_bias": down_bias, "cotangent": cotangent}


@jax.custom_vjp
def low(v):
    return lax.optimization_barrier(v.astype(jnp.bfloat16)).astype(jnp.float32)

@jax.custom_vjp
def low_back(v):
    return v

def low_keep(v):
    return (low(v), None)

def low_pass(kept, grad):
    return (grad,)

def back_keep(v):
    return (v, None)

def back_low(kept, grad):
    return (low(grad),)
low.defvjp(low_keep, low_pass)
low_back.defvjp(back_keep, back_low)
HIGH = lax.Precision.HIGHEST
EPSILON = 1e-06
SLOPE = math.sqrt(2.0 / math.pi)
CUBIC = 0.044715

def layer_norm(features, norm_gain, norm_shift):
    centered = features - lax.optimization_barrier(jnp.mean(features, axis=-1, keepdims=True))
    spread = lax.optimization_barrier(jnp.mean(centered * centered, axis=-1, keepdims=True))
    return centered * lax.rsqrt(spread + EPSILON) * norm_gain + norm_shift

def smooth_gate(features):
    return 0.5 * features * (1.0 + jnp.tanh(SLOPE * (features + CUBIC * features * features * features)))

def layer(inputs, segment_block, params):
    first_gain, first_shift, qkv_weight, query_bias, value_bias, out_weight, out_bias, second_gain, second_shift, up_weight, up_bias, down_weight, down_bias = params
    batch_rows, seq_length, model_width = inputs.shape
    head_shape = (batch_rows, seq_length, HEADS, HDIM)
    normed = low(layer_norm(inputs, first_gain, first_shift))
    mixed_qkv = jnp.einsum('bsd,de->bse', normed, qkv_weight, precision=HIGH)
    queries = low(low_back(mixed_qkv[:, :, :model_width] + query_bias)).reshape(head_shape)
    key_rows = low(low_back(mixed_qkv[:, :, model_width:2 * model_width])).reshape(head_shape)
    values = low(low_back(mixed_qkv[:, :, 2 * model_width:] + value_bias)).reshape(head_shape)
    score_scale = 1.0 / math.sqrt(HDIM)
    scores = low_back(jnp.einsum('bqhd,bkhd->bhqk', queries, key_rows, precision=HIGH) * score_scale)
    same_image = segment_block[:, None, :, None] == segment_block[:, None, None, :]
    scores = jnp.where(same_image, scores, -1e+30)
    row_top = lax.optimization_barrier(jnp.max(scores, axis=-1, keepdims=True))
    exponent = jnp.exp(scores - row_top)
    probability = low(exponent / lax.optimization_barrier(jnp.sum(exponent, axis=-1, keepdims=True)))
    attended = jnp.einsum('bhqk,bkhd->bqhd', probability, values, precision=HIGH)
    attended = low(low_back(attended.reshape(batch_rows, seq_length, model_width)))
    hidden = inputs + low_back(jnp.einsum('bsd,de->bse', attended, out_weight, precision=HIGH) + out_bias)
    normed_two = low(layer_norm(hidden, second_gain, second_shift))
    upward = low_back(jnp.einsum('bsd,df->bsf', normed_two, up_weight, precision=HIGH) + up_bias)
    active = low(smooth_gate(upward))
    return hidden + low_back(jnp.einsum('bsf,fd->bsd', active, down_weight, precision=HIGH) + down_bias)

def reference(tokens, segments, first_gain, first_shift, qkv_weight, query_bias, value_bias, out_weight, out_bias, second_gain, second_shift, up_weight, up_bias, down_weight, down_bias, cotangent):
    params = tuple((weight_item.astype(jnp.float32) for weight_item in (first_gain, first_shift, qkv_weight, query_bias, value_bias, out_weight, out_bias, second_gain, second_shift, up_weight, up_bias, down_weight, down_bias)))
    group_size = math.gcd(SEQS, max(1, 4096 // SEQ))
    blocks = SEQS // group_size
    token_blocks = tokens.reshape(blocks, group_size, SEQ, D)
    segment_blocks = segments.reshape(blocks, group_size, SEQ)
    cot_blocks = cotangent.reshape(blocks, group_size, SEQ, D)

    def accumulate(totals, pieces):
        token_block, segment_block, cot_block = pieces

        def forward(inputs, weights):
            return layer(inputs, segment_block, weights)
        result, pullback = jax.vjp(forward, token_block.astype(jnp.float32), params)
        token_grad, weight_grads = pullback(cot_block.astype(jnp.float32))
        totals = tuple((earlier + later for earlier, later in zip(totals, weight_grads)))
        return (totals, (result.astype(jnp.bfloat16), token_grad))
    zeros_init = tuple((jnp.zeros_like(weight_item) for weight_item in params))
    totals, (outputs, token_grads) = lax.scan(accumulate, zeros_init, (token_blocks, segment_blocks, cot_blocks))
    grad_a, grad_b, grad_c, grad_d, grad_e, grad_f, grad_g, grad_h, grad_i, grad_j, grad_k, grad_l, grad_m = totals
    return (outputs.reshape(SEQS, SEQ, D), token_grads.reshape(SEQS, SEQ, D), grad_a, grad_b, grad_c, grad_d, grad_e, grad_f, grad_g, grad_h, grad_i, grad_j, grad_k, grad_l, grad_m)
```

```python
import functools
import math

import jax
import jax.numpy as jnp
from jax import lax
from jax.experimental import pallas as pl
from jax.experimental.pallas import tpu as pltpu
from jax.sharding import PartitionSpec as P

HEADS = 12


EPSILON = 1e-06
SLOPE = math.sqrt(2.0 / math.pi)
CUBIC = 0.044715


def product(left_side, right_side):
    return jnp.dot(left_side, right_side, preferred_element_type=jnp.float32)


def product_left_turned(left_side, right_side):
    return lax.dot_general(
        left_side, right_side, (((0,), (0,)), ((), ())), preferred_element_type=jnp.float32
    )


def product_right_turned(left_side, right_side):
    return lax.dot_general(
        left_side, right_side, (((1,), (1,)), ((), ())), preferred_element_type=jnp.float32
    )


def norm_forward(features, norm_gain, norm_shift):
    centered = features - jnp.mean(features, axis=-1, keepdims=True)
    inv_spread = lax.rsqrt(jnp.mean(centered * centered, axis=-1, keepdims=True) + EPSILON)
    unit_rows = centered * inv_spread
    return (unit_rows * norm_gain + norm_shift, unit_rows, inv_spread)


def norm_backward(grad_normed, unit_rows, inv_spread, norm_gain):
    scaled = grad_normed * norm_gain
    inner = (
        scaled
        - jnp.mean(scaled, axis=-1, keepdims=True)
        - unit_rows * jnp.mean(scaled * unit_rows, axis=-1, keepdims=True)
    )
    return (
        inner * inv_spread,
        jnp.sum(grad_normed * unit_rows, axis=0),
        jnp.sum(grad_normed, axis=0),
    )


def smooth_gate(features):
    return (
        0.5
        * features
        * (1.0 + jnp.tanh(SLOPE * (features + CUBIC * features * features * features)))
    )


def gate_slope(features):
    bent = jnp.tanh(SLOPE * (features + CUBIC * features * features * features))
    return 0.5 * (1.0 + bent) + 0.5 * features * (1.0 - bent * bent) * SLOPE * (
        1.0 + 3.0 * CUBIC * features * features
    )


def masked_scores(queries, key_rows, same_image, score_scale):
    scores = (
        jnp.einsum("qhd,khd->hqk", queries, key_rows, preferred_element_type=jnp.float32)
        * score_scale
    )
    return jnp.where(same_image[None], scores, -1e30)


def attend_forward(queries, key_rows, values, same_image, score_scale):
    step_heads = queries.shape[1] // 4
    outputs = []
    totals = []
    for head_block in range(4):
        head_span = slice(head_block * step_heads, (head_block + 1) * step_heads)
        scores = masked_scores(
            queries[:, head_span], key_rows[:, head_span], same_image, score_scale
        )
        row_top = jnp.max(scores, axis=-1, keepdims=True)
        exponent = jnp.exp(scores - row_top)
        row_total = jnp.sum(exponent, axis=-1, keepdims=True)
        weights_low = (exponent / row_total).astype(jnp.bfloat16)
        outputs.append(
            jnp.einsum(
                "hqk,khd->qhd",
                weights_low,
                values[:, head_span],
                preferred_element_type=jnp.float32,
            )
        )
        totals.append(row_top + jnp.log(row_total))
    return (jnp.concatenate(outputs, axis=1), totals)


def attend_backward(queries, key_rows, values, same_image, score_scale, totals, grad_attended):
    step_heads = queries.shape[1] // 4
    query_parts = []
    key_parts = []
    value_parts = []
    for head_block in range(4):
        head_span = slice(head_block * step_heads, (head_block + 1) * step_heads)
        scores = masked_scores(
            queries[:, head_span], key_rows[:, head_span], same_image, score_scale
        )
        probability = jnp.exp(scores - totals[head_block])
        grad_piece = grad_attended[:, head_span]
        grad_values = jnp.einsum(
            "hqk,qhd->khd",
            probability.astype(jnp.bfloat16),
            grad_piece,
            preferred_element_type=jnp.float32,
        )
        grad_probs = jnp.einsum(
            "qhd,khd->hqk", grad_piece, values[:, head_span], preferred_element_type=jnp.float32
        )
        grad_scores = (
            probability * (grad_probs - jnp.sum(grad_probs * probability, axis=-1, keepdims=True))
        ).astype(jnp.bfloat16)
        grad_queries = (
            jnp.einsum(
                "hqk,khd->qhd",
                grad_scores,
                key_rows[:, head_span],
                preferred_element_type=jnp.float32,
            )
            * score_scale
        )
        grad_keys = (
            jnp.einsum(
                "hqk,qhd->khd",
                grad_scores,
                queries[:, head_span],
                preferred_element_type=jnp.float32,
            )
            * score_scale
        )
        query_parts.append(grad_queries.astype(jnp.bfloat16))
        key_parts.append(grad_keys.astype(jnp.bfloat16))
        value_parts.append(grad_values.astype(jnp.bfloat16))
    return (
        jnp.concatenate(query_parts, axis=1),
        jnp.concatenate(key_parts, axis=1),
        jnp.concatenate(value_parts, axis=1),
    )


def per_device_plain(
    tokens,
    segments,
    first_gain,
    first_shift,
    qkv_weight,
    query_bias,
    value_bias,
    out_weight,
    out_bias,
    second_gain,
    second_shift,
    up_weight,
    up_bias,
    down_weight,
    down_bias,
    cotangent,
):
    head_count = HEADS
    model_width = tokens.shape[2]
    head_width = model_width // head_count
    score_scale = 1.0 / math.sqrt(head_width)
    gain_one, shift_one, qkv_full, query_shift, value_shift, out_full, out_shift = (
        lax.all_gather(first_gain, "fsdp", axis=0, tiled=True),
        lax.all_gather(first_shift, "fsdp", axis=0, tiled=True),
        lax.all_gather(qkv_weight, "fsdp", axis=0, tiled=True),
        lax.all_gather(query_bias, "fsdp", axis=0, tiled=True),
        lax.all_gather(value_bias, "fsdp", axis=0, tiled=True),
        lax.all_gather(out_weight, "fsdp", axis=0, tiled=True),
        lax.all_gather(out_bias, "fsdp", axis=0, tiled=True),
    )
    gain_two, shift_two, up_full, up_shift, down_full, down_shift = (
        lax.all_gather(second_gain, "fsdp", axis=0, tiled=True),
        lax.all_gather(second_shift, "fsdp", axis=0, tiled=True),
        lax.all_gather(up_weight, "fsdp", axis=0, tiled=True),
        lax.all_gather(up_bias, "fsdp", axis=0, tiled=True),
        lax.all_gather(down_weight, "fsdp", axis=0, tiled=True),
        lax.all_gather(down_bias, "fsdp", axis=0, tiled=True),
    )
    first_scale = gain_one.astype(jnp.float32)
    first_offset = shift_one.astype(jnp.float32)
    second_scale = gain_two.astype(jnp.float32)
    second_offset = shift_two.astype(jnp.float32)
    query_offset = query_shift.astype(jnp.float32)
    value_offset = value_shift.astype(jnp.float32)
    out_offset = out_shift.astype(jnp.float32)
    up_offset = up_shift.astype(jnp.float32)
    down_offset = down_shift.astype(jnp.float32)
    micro_count = tokens.shape[0]
    saved = []
    outputs_low = []
    for batch_index in range(micro_count):
        inputs = tokens[batch_index].astype(jnp.float32)
        segment_row = segments[batch_index]
        same_image = segment_row[:, None] == segment_row[None, :]
        normed, unit_one, spread_one = norm_forward(inputs, first_scale, first_offset)
        normed_low = normed.astype(jnp.bfloat16)
        mixed_qkv = product(normed_low, qkv_full)
        queries = (
            (mixed_qkv[:, :model_width] + query_offset)
            .astype(jnp.bfloat16)
            .reshape(-1, head_count, head_width)
        )
        key_rows = (
            mixed_qkv[:, model_width : 2 * model_width]
            .astype(jnp.bfloat16)
            .reshape(-1, head_count, head_width)
        )
        values = (
            (mixed_qkv[:, 2 * model_width :] + value_offset)
            .astype(jnp.bfloat16)
            .reshape(-1, head_count, head_width)
        )
        attended, totals = attend_forward(queries, key_rows, values, same_image, score_scale)
        attended_low = attended.reshape(-1, model_width).astype(jnp.bfloat16)
        hidden = inputs + (product(attended_low, out_full) + out_offset)
        normed_two, unit_two, spread_two = norm_forward(hidden, second_scale, second_offset)
        normed_two_low = normed_two.astype(jnp.bfloat16)
        upward = product(normed_two_low, up_full) + up_offset
        active_low = smooth_gate(upward).astype(jnp.bfloat16)
        result = hidden + (product(active_low, down_full) + down_offset)
        outputs_low.append(result.astype(jnp.bfloat16))
        saved.append(
            (
                same_image,
                unit_one,
                spread_one,
                normed_low,
                queries,
                key_rows,
                values,
                totals,
                attended_low,
                unit_two,
                spread_two,
                normed_two_low,
                upward,
                active_low,
            )
        )
    gain_two_back, up_back, down_back = (
        lax.all_gather(second_gain, "fsdp", axis=0, tiled=True),
        lax.all_gather(up_weight, "fsdp", axis=0, tiled=True),
        lax.all_gather(down_weight, "fsdp", axis=0, tiled=True),
    )
    gain_one_back, qkv_back, out_back = (
        lax.all_gather(first_gain, "fsdp", axis=0, tiled=True),
        lax.all_gather(qkv_weight, "fsdp", axis=0, tiled=True),
        lax.all_gather(out_weight, "fsdp", axis=0, tiled=True),
    )
    first_scale_back = gain_one_back.astype(jnp.float32)
    second_scale_back = gain_two_back.astype(jnp.float32)
    accum = [
        jnp.zeros(item_array.shape, jnp.float32)
        for item_array in (
            gain_one,
            shift_one,
            qkv_full,
            query_shift,
            value_shift,
            out_full,
            out_shift,
            gain_two,
            shift_two,
            up_full,
            up_shift,
            down_full,
            down_shift,
        )
    ]
    grads_back = []
    for batch_index in range(micro_count):
        (
            same_image,
            unit_one,
            spread_one,
            normed_low,
            queries,
            key_rows,
            values,
            totals,
            attended_low,
            unit_two,
            spread_two,
            normed_two_low,
            upward,
            active_low,
        ) = saved[batch_index]
        grad_down = cotangent[batch_index]
        grad_top = grad_down.astype(jnp.float32)
        down_term = product_left_turned(active_low, grad_down)
        grad_active = product_right_turned(grad_down, down_back)
        grad_up = (grad_active * gate_slope(upward)).astype(jnp.bfloat16)
        up_term = product_left_turned(normed_two_low, grad_up)
        grad_normed_two = product_right_turned(grad_up, up_back)
        hidden_part, gain_two_term, shift_two_term = norm_backward(
            grad_normed_two, unit_two, spread_two, second_scale_back
        )
        grad_hidden = grad_top + hidden_part
        grad_branch = grad_hidden.astype(jnp.bfloat16)
        out_term = product_left_turned(attended_low, grad_branch)
        grad_attended = (
            product_right_turned(grad_branch, out_back)
            .astype(jnp.bfloat16)
            .reshape(-1, head_count, head_width)
        )
        grad_queries, grad_keys, grad_values = attend_backward(
            queries, key_rows, values, same_image, score_scale, totals, grad_attended
        )
        grad_queries = grad_queries.reshape(-1, model_width)
        grad_keys = grad_keys.reshape(-1, model_width)
        grad_values = grad_values.reshape(-1, model_width)
        grad_mixed = jnp.concatenate([grad_queries, grad_keys, grad_values], axis=1)
        qkv_term = product_left_turned(normed_low, grad_mixed)
        grad_normed = product_right_turned(grad_mixed, qkv_back)
        input_part, gain_one_term, shift_one_term = norm_backward(
            grad_normed, unit_one, spread_one, first_scale_back
        )
        grads_back.append(grad_hidden + input_part)
        terms = (
            gain_one_term,
            shift_one_term,
            qkv_term,
            jnp.sum(grad_queries.astype(jnp.float32), axis=0),
            jnp.sum(grad_values.astype(jnp.float32), axis=0),
            out_term,
            jnp.sum(grad_branch.astype(jnp.float32), axis=0),
            gain_two_term,
            shift_two_term,
            up_term,
            jnp.sum(grad_up.astype(jnp.float32), axis=0),
            down_term,
            jnp.sum(grad_top, axis=0),
        )
        accum = [earlier + later for earlier, later in zip(accum, terms)]
    shares = (
        lax.psum_scatter(accum[0], ("fsdp", "dp"), scatter_dimension=0, tiled=True),
        lax.psum_scatter(accum[1], ("fsdp", "dp"), scatter_dimension=0, tiled=True),
        lax.psum_scatter(accum[2], ("fsdp", "dp"), scatter_dimension=0, tiled=True),
        lax.psum_scatter(accum[3], ("fsdp", "dp"), scatter_dimension=0, tiled=True),
        lax.psum_scatter(accum[4], ("fsdp", "dp"), scatter_dimension=0, tiled=True),
        lax.psum_scatter(accum[5], ("fsdp", "dp"), scatter_dimension=0, tiled=True),
        lax.psum_scatter(accum[6], ("fsdp", "dp"), scatter_dimension=0, tiled=True),
        lax.psum_scatter(accum[7], ("fsdp", "dp"), scatter_dimension=0, tiled=True),
        lax.psum_scatter(accum[8], ("fsdp", "dp"), scatter_dimension=0, tiled=True),
        lax.psum_scatter(accum[9], ("fsdp", "dp"), scatter_dimension=0, tiled=True),
        lax.psum_scatter(accum[10], ("fsdp", "dp"), scatter_dimension=0, tiled=True),
        lax.psum_scatter(accum[11], ("fsdp", "dp"), scatter_dimension=0, tiled=True),
        lax.psum_scatter(accum[12], ("fsdp", "dp"), scatter_dimension=0, tiled=True),
    )
    return (
        jnp.stack(outputs_low),
        jnp.stack(grads_back),
        shares[0],
        shares[1],
        shares[2],
        shares[3],
        shares[4],
        shares[5],
        shares[6],
        shares[7],
        shares[8],
        shares[9],
        shares[10],
        shares[11],
        shares[12],
    )


MESH = pl.DeviceIdType.MESH

class Place:
    def __init__(s, nz):
        s.nz = nz
        s.f = lax.axis_index("fsdp"); s.c = lax.axis_index("dp")
        s.z = s.f // 4
        s.p = s.f % 4
        x = s.f % 2; y = (s.f // 2) % 2
        a = jnp.where(s.c == 0, x, y); b = jnp.where(s.c == 0, y, x)
        sa = jnp.where(s.c == 0, 1, 2); sb = jnp.where(s.c == 0, 2, 1)
        s.pa = s.p + (1 - 2 * a) * sa
        s.pb = s.p + (1 - 2 * b) * sb
        s.pab = s.pa + (1 - 2 * b) * sb
    def at(s, z, p, c=None):
        return {"fsdp": z * 4 + p, "dp": s.c if c is None else c}

def barrier(pc):
    bar = pltpu.get_barrier_semaphore()
    def sig(z, p, c=None):
        pl.semaphore_signal(bar, inc=1, device_id=pc.at(z, p, c), device_id_type=MESH)
    sig(pc.z, pc.pa); sig(pc.z, pc.pb); sig(pc.z, pc.p, 1 - pc.c)
    for d in range(1, pc.nz):
        @pl.when(pc.z >= d)
        def _(): sig(pc.z - d, pc.p)
        @pl.when(pc.z + d < pc.nz)
        def _(): sig(pc.z + d, pc.p)
    pl.semaphore_wait(bar, 3 + pc.nz - 1)

def others(pc, fn):
    for d in range(1, pc.nz):
        @pl.when(pc.z + d < pc.nz)
        def _(): fn(pc.z + d)
        @pl.when(pc.z >= d)
        def _(): fn(pc.z - d)

class Gather:
    def __init__(s, pc, k, kind, view, src, zs, ls, ss, so):
        s.pc, s.k, s.kind, s.view, s.src = pc, k, kind, view, src
        s.zs, s.ls, s.ss, s.so = zs, ls, ss, so
    def rc(s, src, dst, ssem, rsem, dev):
        return pltpu.make_async_remote_copy(src_ref=src, dst_ref=dst, send_sem=ssem, recv_sem=rsem, device_id=dev, device_id_type=MESH)
    def zc(s, z2, zo=None):
        pc = s.pc; v = s.view(pc.z if zo is None else zo, pc.p, pc.c)
        return s.rc(s.src, v, s.ss.at[s.k, z2], s.zs.at[s.k, pc.z if zo is None else zo], pc.at(z2, pc.p))
    def line(s, p, sem, dev, q):
        pc = s.pc; v = s.view(None, p, pc.c)
        return s.rc(v, v, s.so.at[s.k, q], s.ls.at[s.k, sem], dev)
    def a1(s): return s.line(s.pc.p, 0, s.pc.at(s.pc.z, s.pc.pa), 0)
    def b1(s): return s.line(s.pc.p, 1, s.pc.at(s.pc.z, s.pc.pb), 1)
    def b2(s): return s.line(s.pc.pa, 2, s.pc.at(s.pc.z, s.pc.pb), 2)
    def core(s, q):
        pc = s.pc
        return s.line((pc.p, pc.pa, pc.pb, pc.pab)[q], 3 + q, pc.at(pc.z, pc.p, 1 - pc.c), 3 + q)
    def st0(s):
        others(s.pc, lambda z2: s.zc(z2).start())
    def st1(s):
        pc = s.pc
        others(pc, lambda z2: s.zc(z2, zo=z2).wait_recv())
        s.a1().start(); s.b1().start(); s.core(0).start()
    def st2(s):
        s.a1().wait_recv()
        s.b2().start(); s.core(1).start()
    def st3(s):
        s.b1().wait_recv(); s.core(2).start()
    def st4(s):
        s.b2().wait_recv(); s.core(3).start()
    def fin(s):
        for q in range(4): s.core(q).wait_recv()
    def sent(s):
        others(s.pc, lambda z2: s.zc(z2).wait_send())
        s.a1().wait_send(); s.b1().wait_send(); s.b2().wait_send()
        for q in range(4): s.core(q).wait_send()

class GatherMinor(Gather):
    def piece(s, p, sem, dev, q, src=None):
        pc = s.pc; v = s.view(pc.z, p, pc.c)
        return s.rc(v if src is None else src, v, s.so.at[s.k, q], s.ls.at[s.k, sem], dev)
    def a1(s): return s.piece(s.pc.p, 0, s.pc.at(s.pc.z, s.pc.pa), 0, s.src)
    def b1(s): return s.piece(s.pc.p, 1, s.pc.at(s.pc.z, s.pc.pb), 1, s.src)
    def b2(s): return s.piece(s.pc.pa, 2, s.pc.at(s.pc.z, s.pc.pb), 2)
    def zc(s, z2, zo=None):
        pc = s.pc; v = s.view(pc.z if zo is None else zo, None, pc.c)
        return s.rc(v, v, s.ss.at[s.k, z2], s.zs.at[s.k, pc.z if zo is None else zo], pc.at(z2, pc.p))
    def corez(s, z):
        pc = s.pc; v = s.view(z, None, pc.c)
        return s.rc(v, v, s.so.at[s.k, 3 + z], s.ls.at[s.k, 3 + z], pc.at(pc.z, pc.p, 1 - pc.c))
    def st0(s):
        s.a1().start(); s.b1().start()
    def st1(s):
        s.a1().wait_recv(); s.b2().start()
    def st2(s):
        s.b1().wait_recv(); s.b2().wait_recv()
        others(s.pc, lambda z2: s.zc(z2).start())
        s.corez(s.pc.z).start()
    def st3(s):
        pass
    def st4(s):
        def go(z2):
            s.zc(z2, zo=z2).wait_recv(); s.corez(z2).start()
        others(s.pc, go)
    def fin(s):
        for z in range(s.pc.nz): s.corez(z).wait_recv()
    def sent(s):
        others(s.pc, lambda z2: s.zc(z2).wait_send())
        s.a1().wait_send(); s.b1().wait_send(); s.b2().wait_send()
        for z in range(s.pc.nz): s.corez(z).wait_send()
BF=jnp.bfloat16; F32=jnp.float32
EPS=EPSILON

class GatherVec(Gather):
    def a1(s): return s.line(s.pc.p, 0, s.pc.at(s.pc.z, s.pc.pa), 0)
    def st1(s):
        pc = s.pc
        others(pc, lambda z2: s.zc(z2, zo=z2).wait_recv())
        s.a1().start(); s.b1().start()
    def st2(s):
        s.a1().wait_recv(); s.b2().start()
    def st3(s): s.b1().wait_recv()
    def st4(s): s.b2().wait_recv()
    def fin(s): pass
    def sent(s):
        others(s.pc, lambda z2: s.zc(z2).wait_send())
        s.a1().wait_send(); s.b1().wait_send(); s.b2().wait_send()

class GatherMinorR(GatherMinor):
    def up(s, zo):
        pc=s.pc; v=s.view(zo,None,pc.c)
        return s.rc(v,v,s.ss.at[s.k,zo],s.zs.at[s.k,zo],pc.at(pc.z+1,pc.p))
    def dn(s, zo):
        pc=s.pc; v=s.view(zo,None,pc.c)
        return s.rc(v,v,s.so.at[s.k,7+zo],s.zs.at[s.k,zo],pc.at(pc.z-1,pc.p))
    def st2(s):
        pc=s.pc
        s.b1().wait_recv(); s.b2().wait_recv()
        @pl.when(pc.z<pc.nz-1)
        def _(): s.up(pc.z).start()
        @pl.when(pc.z>0)
        def _(): s.dn(pc.z).start()
        s.corez(pc.z).start()
    def relay(s,d):
        pc=s.pc
        @pl.when(pc.z>=d)
        def _():
            s.up(pc.z-d).wait_recv()
            @pl.when(pc.z<pc.nz-1)
            def _(): s.up(pc.z-d).start()
            s.corez(pc.z-d).start()
        @pl.when(pc.z+d<pc.nz)
        def _():
            s.up(pc.z+d).wait_recv()
            @pl.when(pc.z>0)
            def _(): s.dn(pc.z+d).start()
            s.corez(pc.z+d).start()
    def st3(s): s.relay(1)
    def st4(s):
        for d in range(2,s.pc.nz): s.relay(d)
    def sent(s):
        pc=s.pc
        for d in range(pc.nz):
            @pl.when((pc.z>=d)&(pc.z<pc.nz-1))
            def _(): s.up(pc.z-d).wait_send()
            @pl.when((pc.z+d<pc.nz)&(pc.z>0))
            def _(): s.dn(pc.z+d).wait_send()
        s.a1().wait_send(); s.b1().wait_send(); s.b2().wait_send()
        for z in range(s.pc.nz): s.corez(z).wait_send()

def dotT(a,b): return lax.dot_general(a,b,(((1,),(1,)),((),())),preferred_element_type=F32)
def dot(a,b): return jnp.dot(a,b,preferred_element_type=F32)
def dotL(a,b): return lax.dot_general(a,b,(((0,),(0,)),((),())),preferred_element_type=F32)

def loop(n, body, events=()):
    ev={}
    for i,fn in events: ev.setdefault(min(i,n-1),[]).append(fn)
    def step(i,_):
        body(i)
        for j in sorted(ev):
            @pl.when(i==j)
            def _():
                for fn in ev[j]: fn()
        return 0
    lax.fori_loop(0,n,step,0)

def norm(x, g, b):
    mean=jnp.mean(x,axis=-1,keepdims=True)
    cen=x-mean
    inv=lax.rsqrt(jnp.mean(cen*cen,axis=-1,keepdims=True)+EPS)
    return (cen*inv)*g+b

def chunks(D, FF, down_rows):
    h=down_rows//2
    return [(0,0,None,0,D,'M'),(0,0,None,2*D,D//2,'M'),(1,0,None,0,D//2,'M'),(2,0,None,0,FF//4,'M'),(2,0,None,FF//2,FF//4,'M'),(3,0,h,0,D//2,'M'),(3,h,h,0,D//2,'N')]

def k1_body(D,FF,H,NZ,nseq,S,ev_lag, *refs):
    (tok,segr,slab,wq,wo,wu,wd,
     out_h,qkv_h,pt_h,att_h,hid_h,n1_h,n2_h,act_h,slp_h,gq_h,go_h,gu_h,gd_h,vec_h,
     gq,go,gu,gd,vbuf,n1,qkv,att,hid,n2,act,slp,outb,pst,bias,vec,upb,n1t,n2t,attt,actt,
     zs,lsem,ss,so,loc,hsem,psem)=refs
    R=nseq*S
    pc=Place(NZ)
    bufs=[gq,go,gu,gd]; ws=[wq,wo,wu,wd]
    CH=chunks(D,FF,wd.shape[0])
    gs=[]; own=[]
    for k,(wi,r0,nr,c0,ncol,kind) in enumerate(CH):
        nr=ws[wi].shape[0] if nr is None else nr
        def view(z,p,c,wi=wi,r0=r0,nr=nr,c0=c0,ncol=ncol):
            zi=slice(None) if z is None else z
            pi=slice(None) if p is None else p
            return bufs[wi].at[zi,pi,pl.ds(r0,nr),pl.ds(pl.multiple_of(c*ncol+c0,128),ncol)]
        src=ws[wi].at[pl.ds(r0,nr),pl.ds(pl.multiple_of(pc.c*ncol+c0,128),ncol)]
        gs.append((Gather if kind=='M' else GatherMinorR)(pc,k,kind,view,src,zs,lsem,ss,so))
        cp=pltpu.make_async_copy(src, view(pc.z,pc.p,pc.c), loc.at[k]); cp.start(); own.append(cp)
    def vview(z,p,c):
        return vbuf.at[slice(None) if z is None else z, slice(None) if p is None else p]
    kv=len(CH)
    gv=GatherVec(pc,kv,'V',vview,slab,zs,lsem,ss,so)
    cp=pltpu.make_async_copy(slab, vview(pc.z,pc.p,pc.c), loc.at[kv]); cp.start(); own.append(cp)
    barrier(pc)
    gv.st0(); gs[0].st0()
    gs[6].st0()
    for k in range(1,6): gs[k].st0()
    for cp in own: cp.wait()
    sends=[]
    def put(src,dst,sem):
        c=pltpu.make_async_copy(src,dst,sem); c.start(); sends.append(c)
    for q in range(nseq):
        row=jnp.broadcast_to(segr[q:q+1,:],(S,S))
        bias[q]=jnp.where(row==row.T,0.0,-1e30).astype(F32)
    gv.st1(); gs[0].st1(); gs[6].st1(); gs[1].st1()
    gv.st2(); gv.st3(); gs[0].st2(); gs[0].st3(); gv.st4()
    rows=[vbuf[i//4,i%4] for i in range(4*NZ)]
    nv=D//(4*NZ)
    vec[...]=jnp.concatenate([r[:,:nv] for r in rows],axis=1)
    upb[...]=jnp.concatenate([jnp.concatenate([r[8:9,:],r[9:10,:FF//(4*NZ)-128]],axis=1) for r in rows],axis=1)
    gs[6].st2(); gs[1].st2(); gs[2].st1()
    BR=128
    def n1b(i):
        r=pl.ds(pl.multiple_of(i*BR,BR),BR)
        y=norm(tok[r,:].astype(F32),vec[0:1,:],vec[1:2,:]).astype(BF)
        n1[r,:]=y
        n1t[:,r]=y.T
    loop(R//BR,n1b)
    gs[0].st4(); gs[1].st3(); gs[3].st1(); gs[2].st2()
    put(n1t,n1_h,hsem.at[0]); put(vec,vec_h,hsem.at[1])
    gs[0].fin()
    TN=256
    def qk(j):
        c=pl.ds(pl.multiple_of(j*TN,TN),TN)
        w=gq[:,:,:,c].reshape(D,TN)
        y=dot(n1[...],w)
        nq=D//TN
        cb=pl.ds(pl.multiple_of((j%nq)*TN,TN),TN)
        b=jnp.where(j<nq,vec[2:3,cb],jnp.where(j<2*nq,0.0,vec[3:4,cb]))
        qkv[pl.ds(pl.multiple_of((j//nq)*R,128),R),cb]=(y+b).astype(BF)
    loop(2*D//TN,qk)
    gs[1].st4(); gs[2].st3(); gs[3].st2(); gs[4].st1()
    gs[1].fin()
    loop(D//TN,lambda j: qk(j+2*D//TN))
    put(qkv,qkv_h,hsem.at[3])
    put(gq,gq_h,hsem.at[4])
    gs[2].st4()
    HP=H//2
    lane=lax.broadcasted_iota(jnp.int32,(1,128),1)
    def attn(i):
        s=i//HP; hp=i%HP
        r=pl.ds(pl.multiple_of(s*S,128),S)
        hc=pl.ds(pl.multiple_of(hp*128,128),128)
        q2,k2,v2=[qkv[pl.ds(pl.multiple_of(w*R+s*S,128),S),hc] for w in range(3)]
        vT=v2.T
        sl=i%2
        @pl.when(i>=2)
        def _(): pltpu.make_async_copy(pst.at[sl],pt_h.at[i-2],psem.at[sl]).wait()
        os_=[]
        for h in range(2):
            qm=jnp.where((lane>=64) if h else (lane<64),q2*BF(0.125),BF(0))
            sT=dotT(k2,qm)+bias[s]
            m=jnp.max(sT,axis=0,keepdims=True)
            e=jnp.exp(sT-m)
            l=jnp.sum(e,axis=0,keepdims=True)
            p=(e*(1.0/l)).astype(BF)
            pst[sl,h]=p
            os_.append(dot(vT[64*h:64*h+64],p))
        oT=jnp.concatenate(os_,axis=0).astype(BF)
        attt[hc,r]=oT
        att[r,hc]=oT.T
        pltpu.make_async_copy(pst.at[sl],pt_h.at[i],psem.at[sl]).start()
    loop(2*HP if nseq==2 else nseq*HP,attn,[(0,gs[3].st3),(1,gs[4].st2),(2,gs[5].st1),(4,gs[3].st4),(5,gs[6].st3),(6,gs[4].st3),(8,gs[5].st2),(9,gs[4].st4)])
    put(attt,att_h,hsem.at[5])
    gs[2].fin()
    put(go,go_h,hsem.at[6])
    def op(j):
        c=pl.ds(pl.multiple_of(j*TN,TN),TN)
        w=go[:,:,:,c].reshape(D,TN)
        hid[:,c]=dot(att[...],w)+vec[4:5,c]+tok[:,c].astype(F32)
    loop(D//TN,op)
    put(hid,hid_h,hsem.at[7])
    gs[5].st3()
    def n2b(i):
        r=pl.ds(pl.multiple_of(i*BR,BR),BR)
        y=norm(hid[r,:],vec[5:6,:],vec[6:7,:]).astype(BF)
        n2[r,:]=y
        n2t[:,r]=y.T
    loop(R//BR,n2b)
    put(n2t,n2_h,hsem.at[8])
    gs[3].fin()
    def upj(j):
        c=pl.ds(pl.multiple_of(j*TN,TN),TN)
        w=gu[:,:,:,c].reshape(D,TN)
        u=dot(n2[...],w)+upb[:,c]
        u2=u*u
        t=jnp.tanh(SLOPE*(u+CUBIC*u*u2))
        hp1=0.5*(1.0+t)
        a=(u*hp1).astype(BF)
        act[:,c]=a
        actt[c,:]=a.T
        slp[:,c]=(hp1+0.5*u*(1.0-t*t)*(SLOPE*(1.0+3.0*CUBIC*u2))).astype(BF)
    loop(FF//2//TN,upj,[(2,gs[5].st4)])
    gs[4].fin()
    put(gu,gu_h,hsem.at[9])
    loop(FF//2//TN,lambda j: upj(j+FF//2//TN),[(2,gs[6].st4)])
    put(actt,act_h,hsem.at[10]); put(slp,slp_h,hsem.at[11])
    gs[5].fin(); gs[6].fin()
    put(gd,gd_h,hsem.at[12])
    def dn(j):
        c=pl.ds(pl.multiple_of(j*TN,TN),TN)
        w=gd[:,:,:,c].reshape(FF,TN)
        outb[:,c]=(dot(act[...],w)+vec[7:8,c]+hid[:,c]).astype(BF)
    loop(D//TN,dn)
    put(outb,out_h,hsem.at[13])
    n=nseq*HP
    for i in (n-2,n-1):
        pltpu.make_async_copy(pst.at[i%2],pt_h.at[i],psem.at[i%2]).wait()
    for g in gs: g.sent()
    gv.sent()
    for c in sends: c.wait()

def k1_call(tok,segr,slab,wq,wo,wu,wd,D,FF,H,NZ):
    nseq,S=tok.shape[0],tok.shape[1]
    R=nseq*S
    sds=jax.ShapeDtypeStruct
    g4=[(NZ,4)+w.shape for w in (wq,wo,wu,wd)]
    outs=[sds((R,D),BF),sds((3*R,D),BF),sds((nseq*H//2,2,S,S),BF),sds((D,R),BF),sds((R,D),F32),sds((D,R),BF),sds((D,R),BF),sds((FF,R),BF),sds((R,FF),BF)]+[sds(g,BF) for g in g4]+[sds((16,D),F32)]
    V=pltpu.VMEM
    n=8
    scr=[V(g,BF) for g in g4]+[V((NZ,4,16,128),F32),V((R,D),BF),V((3*R,D),BF),V((R,D),BF),V((R,D),F32),V((R,D),BF),V((R,FF),BF),V((R,FF),BF),V((R,D),BF),V((2,2,S,S),BF),V((nseq,S,S),F32),V((16,D),F32),V((1,FF),F32),V((D,R),BF),V((D,R),BF),V((D,R),BF),V((FF,R),BF)]
    dma=pltpu.SemaphoreType.DMA
    scr+=[dma((n,NZ)),dma((n,7)),dma((n,NZ)),dma((n,7+NZ)),dma((n,)),dma((14,)),dma((2,))]
    vm=pl.BlockSpec(memory_space=pltpu.VMEM); anyb=pl.BlockSpec(memory_space=pl.ANY)
    flops=2*R*D*(4*D+2*FF)
    return pl.pallas_call(functools.partial(k1_body,D,FF,H,NZ,nseq,S,1),
        out_shape=outs,in_specs=[vm]*7,out_specs=[anyb]*len(outs),scratch_shapes=scr,name="gather_forward",
        compiler_params=pltpu.CompilerParams(collective_id=0,has_side_effects=True,vmem_limit_bytes=63*1024*1024))(
        tok.reshape(R,D),segr,slab,wq,wo,wu,wd)

def make_slab(vs, upb):
    m=vs[0].shape[0]; L=upb.shape[0]
    rows=[jnp.pad(v.astype(F32)[None],((0,0),(0,128-m))) for v in vs]
    u=upb.astype(F32)
    rows.append(u[None,:128]); rows.append(jnp.pad(u[None,128:],((0,0),(0,256-L))))
    return jnp.pad(jnp.concatenate(rows,axis=0),((0,6),(0,0)))

class Scatter:
    def __init__(s, pc, k, g, pb_, bb, ab, zb, out, sem, zsem, kv):
        s.pc,s.k,s.g,s.pb_,s.bb,s.ab,s.zb,s.out,s.sem,s.zsem=pc,k,g,pb_,bb,ab,zb,out,sem,zsem
    def rc(s,src,dst,q,dev):
        return pltpu.make_async_remote_copy(src_ref=src,dst_ref=dst,send_sem=s.sem.at[s.k,0,q],recv_sem=s.sem.at[s.k,1,q],device_id=dev,device_id_type=MESH)
    def pair(s):
        pc=s.pc
        return s.rc(s.g.at[1-pc.c], s.pb_, 0, pc.at(pc.z,pc.p,1-pc.c))
    def b(s,w):
        pc=s.pc
        return s.rc(s.g.at[pc.c,:,(pc.pb,pc.pab)[w]], s.bb.at[w], 1+w, pc.at(pc.z,pc.pb))
    def a(s):
        pc=s.pc
        return s.rc(s.g.at[pc.c,:,pc.pa], s.ab, 3, pc.at(pc.z,pc.pa))
    def zc(s,z2):
        pc=s.pc
        return pltpu.make_async_remote_copy(src_ref=s.g.at[pc.c,z2,pc.p],dst_ref=s.zb.at[pc.z],send_sem=s.zsem.at[s.k,0,z2],recv_sem=s.zsem.at[s.k,1,pc.z],device_id=pc.at(z2,pc.p),device_id_type=MESH)
    def zr(s,zo):
        pc=s.pc
        return pltpu.make_async_remote_copy(src_ref=s.g.at[pc.c,zo,pc.p],dst_ref=s.zb.at[zo],send_sem=s.zsem.at[s.k,0,zo],recv_sem=s.zsem.at[s.k,1,zo],device_id=pc.at(zo,pc.p),device_id_type=MESH)
    def stP(s): s.pair().start()
    def stB(s):
        pc=s.pc; s.pair().wait_recv()
        for w,p in enumerate((pc.pb,pc.pab)):
            def add(z,_,p=p):
                s.g[pc.c,z,p]=s.g[pc.c,z,p]+s.pb_[z,p]
                return 0
            lax.fori_loop(0,pc.nz,add,0)
        s.b(0).start(); s.b(1).start()
    def stA(s):
        pc=s.pc; s.b(1).wait_recv()
        def add(z,_):
            s.g[pc.c,z,pc.pa]=(s.g[pc.c,z,pc.pa].astype(F32)+s.pb_[z,pc.pa].astype(F32)+s.bb[1,z].astype(F32)).astype(s.g.dtype)
            return 0
        lax.fori_loop(0,pc.nz,add,0)
        s.a().start()
    def stZ(s):
        pc=s.pc; s.b(0).wait_recv(); s.a().wait_recv()
        def add(z,_):
            s.g[pc.c,z,pc.p]=(s.g[pc.c,z,pc.p].astype(F32)+s.pb_[z,pc.p].astype(F32)+(s.bb[0,z].astype(F32)+s.ab[z].astype(F32))).astype(s.g.dtype)
            return 0
        lax.fori_loop(0,pc.nz,add,0)
        others(pc, lambda z2: s.zc(z2).start())
    def stF(s):
        pc=s.pc
        others(pc, lambda z2: s.zr(z2).wait_recv())
        s.zb[pc.z]=s.g[pc.c,pc.z,pc.p]
        t=s.zb[0].astype(F32)
        for z in range(1,pc.nz): t=t+s.zb[z].astype(F32)
        s.out(t)
    def sent(s):
        s.pair().wait_send(); s.b(0).wait_send(); s.b(1).wait_send(); s.a().wait_send()
        others(s.pc, lambda z2: s.zc(z2).wait_send())

def k2_body(D,FF,H,NZ,nseq,S,*refs):
    (actT_h,cot_h,gd_h,slp_h,n2T_h,gu_h,hid_h,attT_h,go_h,qkv_h,pt_h,gq_h,n1T_h,tok_h,vec_h,
     tg_h,o_q,o_o,o_u,o_d,*rest)=refs
    o_v=rest[:9]
    (actT,cot,gd,slp,n2T,gu,hid,attT,go,vec,pst,dn,br,datt,dqkv,vg,ug,
     gd0,gd1,*rest)=rest[9:]
    (p0,p1,p2,p3,p4,p5,p6,b0,b1,b2,b3,b4,b5,b6,a0,a1,a2,a3,a4,a5,a6,z0,z1,z2,z3,z4,z5,z6,
     gu0,gu1,gout,gv,vgb,vp,vb,va,vz,sem,zsem,lsem,psem,osem)=rest
    R=nseq*S
    pc=Place(NZ)
    qkv,n1T,gq,tok,gqk=actT.at[pl.ds(0,3*R)],actT.at[pl.ds(3*R,R)],gd,n2T,gd0
    names=[actT,cot,gd,slp,n2T,gu,hid,attT,go,qkv,None,n1T,tok,vec]
    srcs=[actT_h,cot_h,gd_h,slp_h,n2T_h,gu_h,hid_h,attT_h,go_h,qkv_h,None,n1T_h,tok_h,vec_h]
    ld={}
    def fetch(*ks):
        for i in ks:
            ld[i]=pltpu.make_async_copy(srcs[i],names[i],lsem.at[i]); ld[i].start()
    need=lambda *ks: [ld[k].wait() for k in ks]
    gqc=[pltpu.make_async_copy(gq_h.at[:,pl.ds(w*D,D)],gq.at[pl.ds(w*D,D)],lsem.at[14+w]) for w in range(3)]
    fetch(0,1,2,3,4,5,6,13,7,8)
    barrier(pc)
    rr=D//(8*NZ); rd=FF//(8*NZ)
    def outd(r0):
        def fn(t):
            for w in range(2): o_d[pl.ds(r0+w*rr,rr),:]=t[:,w*D:(w+1)*D]
        return fn
    def outw(ref,r0,c0):
        def fn(t):
            ref[pl.ds(r0,t.shape[0]),pl.ds(c0,t.shape[1])]=t
        return fn
    HF=FF//2
    sc=[Scatter(pc,0,gd0,p0,b0,a0,z0,outd(0),sem,zsem,0),
        Scatter(pc,1,gd1,p1,b1,a1,z1,outd(rd//2),sem,zsem,0),
        Scatter(pc,2,gu0,p2,b2,a2,z2,outw(o_u,0,0),sem,zsem,0),
        Scatter(pc,3,gu1,p3,b3,a3,z3,outw(o_u,0,HF),sem,zsem,0),
        Scatter(pc,4,gout,p4,b4,a4,z4,outw(o_o,0,0),sem,zsem,0),
        Scatter(pc,5,gqk,p5,b5,a5,z5,outw(o_q,0,0),sem,zsem,0),
        Scatter(pc,6,gv,p6,b6,a6,z6,outw(o_q,0,2*D),sem,zsem,0)]
    TN=256
    lanes=lambda j,w=TN: pl.ds(pl.multiple_of(j*w,128),w)
    vg[...]=jnp.zeros_like(vg)
    need(0,1)
    def l1(i):
        y=dot(actT[pl.ds(pl.multiple_of(i*4*rd,128),4*rd),:],cot[...]).astype(BF)
        for d in range(2):
            for c in range(2):
                for h,g in enumerate((gd0,gd1)):
                    o=(d*2+c)*rd+h*(rd//2)
                    for w in range(2): g[c,i//2,2*(i%2)+d,:,w*D:(w+1)*D]=y[o+w*rr:o+(w+1)*rr]
    loop(2*NZ,l1)
    sc[0].stP(); sc[1].stP()
    fetch(9,11)
    need(2,3)
    def l2(j):
        c=lanes(j)
        da=dotT(cot[...],gd[pl.ds(pl.multiple_of(j*TN,TN),TN),:])
        du=(da*slp[:,c].astype(F32)).astype(BF)
        slp[:,c]=du
        ug[:,c]=jnp.sum(du.astype(F32),axis=0,keepdims=True)
    loop(FF//TN,l2,[(3,sc[0].stB),(6,sc[1].stB)])
    for c in gqc: c.start()
    need(4)
    def scat(g,lhs,rhs,rhs_c,g_c):
        y=dot(lhs[...],rhs[:,rhs_c]).reshape(NZ,4,2,rr,TN)
        for c in range(2):
            for z in range(NZ):
                g[c,z,:,:,g_c]=y[z,:,c].astype(BF)
    nh=HF//TN
    loop(nh,lambda j: scat(gu0,n2T,slp,lanes(j),lanes(j)),[(2,sc[0].stA)])
    sc[2].stP()
    loop(nh,lambda j: scat(gu1,n2T,slp,lanes(j+nh),lanes(j)),[(2,sc[1].stA),(3,sc[2].stB)])
    sc[3].stP()
    fetch(12)
    need(5)
    def l4(j):
        dn[:,lanes(j)]=dotT(slp[...],gu[pl.ds(pl.multiple_of(j*TN,TN),TN),:])
    loop(D//TN,l4,[(0,sc[0].stZ),(1,sc[3].stB)])
    need(6,13)
    BR=128
    def back(x,g,gain,top):
        mean=jnp.mean(x,axis=-1,keepdims=True)
        cen=x-mean
        inv=lax.rsqrt(jnp.mean(cen*cen,axis=-1,keepdims=True)+EPS)
        unit=cen*inv
        sg=g*gain
        inner=sg-jnp.mean(sg,axis=-1,keepdims=True)-unit*jnp.mean(sg*unit,axis=-1,keepdims=True)
        return top+inner*inv, jnp.sum(g*unit,axis=0,keepdims=True), jnp.sum(g,axis=0,keepdims=True)
    def l5(i):
        r=pl.ds(pl.multiple_of(i*BR,BR),BR)
        ct=cot[r,:].astype(F32)
        h,gg,gs=back(hid[r,:],dn[r,:],vec[5:6,:],ct)
        hid[r,:]=h
        hb=h.astype(BF)
        br[r,:]=hb
        vg[5:6,:]+=gg; vg[6:7,:]+=gs
        vg[4:5,:]+=jnp.sum(hb.astype(F32),axis=0,keepdims=True)
        vg[7:8,:]+=jnp.sum(ct,axis=0,keepdims=True)
    loop(R//BR,l5,[(2,sc[1].stZ),(4,sc[2].stA)])
    need(7,8)
    loop(D//TN,lambda j: scat(gout,attT,br,lanes(j),lanes(j)),[(1,sc[0].stF)])
    sc[4].stP()
    def l6(j):
        datt[:,lanes(j)]=dotT(br[...],go[pl.ds(pl.multiple_of(j*TN,TN),TN),:]).astype(BF)
    loop(D//TN,l6,[(0,sc[3].stA),(1,sc[4].stB)])
    need(9)
    HP=H//2
    n=nseq*HP
    lane=lax.broadcasted_iota(jnp.int32,(1,128),1)
    pcopy=lambda i: pltpu.make_async_copy(pt_h.at[i],pst.at[i%2],psem.at[i%2])
    pcopy(0).start()
    def l7(i):
        s=i//HP; hp=i%HP
        r=pl.ds(pl.multiple_of(s*S,128),S)
        c0,c1,c2=[pl.ds(pl.multiple_of(w*D+hp*128,128),128) for w in range(3)]
        pcopy(i).wait()
        @pl.when(i+1<n)
        def _(): pcopy(i+1).start()
        q2,k2,v2=[actT[pl.ds(pl.multiple_of(w*R+s*S,128),S),c0] for w in range(3)]; da=datt[r,c0]
        kT=k2.T
        dq=[];dk=[];dv=[]
        for h in range(2):
            lo=(lane>=64) if h else (lane<64)
            pT=pst[i%2,h]
            dv.append(dot(pT,da))
            dpT=dotT(v2,jnp.where(lo,da,BF(0)))
            pf=pT.astype(F32)
            t=dpT*pf
            ds=(t-pf*jnp.sum(t,axis=0,keepdims=True)).astype(BF)
            dk.append(dot(ds,q2))
            dq.append(dot(kT[64*h:64*h+64],ds))
        dvv=jnp.where(lane<64,dv[0],dv[1]).astype(BF)
        dkk=(jnp.where(lane<64,dk[0],dk[1])*0.125).astype(BF)
        dqq=(jnp.concatenate(dq,axis=0).T*0.125).astype(BF)
        dqkv[r,c0]=dqq; dqkv[r,c1]=dkk; dqkv[r,c2]=dvv
        vg[2:3,c0]+=jnp.sum(dqq.astype(F32),axis=0,keepdims=True)
        vg[3:4,c0]+=jnp.sum(dvv.astype(F32),axis=0,keepdims=True)
    loop(n,l7,[(1,sc[2].stZ),(2,sc[1].stF),(3,sc[4].stA),(5,sc[3].stZ),(6,sc[2].stF),(8,sc[4].stZ),(10,sc[3].stF),(11,sc[4].stF)])
    need(11)
    sc[0].sent()
    nq=D//TN
    loop(2*nq,lambda j: scat(gqk,n1T,dqkv,lanes(j),lanes(j)))
    sc[5].stP()
    loop(nq,lambda j: scat(gv,n1T,dqkv,lanes(j+2*nq),lanes(j)),[(0,sc[5].stB)])
    sc[6].stP()
    for c in gqc: c.wait()
    need(12)
    def l9(j):
        dn[:,lanes(j)]=sum(dotT(dqkv[:,w*D:(w+1)*D],gq[pl.ds(pl.multiple_of(w*D+j*TN,TN),TN),:]) for w in range(3))
    loop(nq,l9,[(0,sc[6].stB)])
    def l10(i):
        r=pl.ds(pl.multiple_of(i*BR,BR),BR)
        t,gg,gs=back(tok[r,:].astype(F32),dn[r,:],vec[0:1,:],hid[r,:])
        dn[r,:]=t
        vg[0:1,:]+=gg; vg[1:2,:]+=gs
    loop(R//BR,l10,[(2,sc[5].stA)])
    oc=pltpu.make_async_copy(dn,tg_h,osem.at[0]); oc.start()
    nv=D//(4*NZ); nu=FF//(4*NZ)
    for i in range(4*NZ):
        for c in range(2):
            vgb[c,i//4,i%4]=jnp.concatenate([jnp.pad(vg[0:8,nv*i+c*(nv//2):nv*i+(c+1)*(nv//2)],((0,0),(0,128-nv//2))),
               jnp.pad(ug[:,nu*i+c*(nu//2):nu*i+(c+1)*(nu//2)],((0,7),(0,128-nu//2)))],axis=0)
    def outv(t):
        for q in range(8): o_v[q][...]=t[q:q+1,:nv//2]
        o_v[8][...]=t[8:9,:nu//2]
    sv=Scatter(pc,7,vgb,vp,vb,va,vz,outv,sem,zsem,0)
    sv.stP()
    sc[6].stA();
    sv.stB(); sc[5].stZ(); sc[6].stZ(); sv.stA(); sv.stZ()
    sc[5].stF(); sc[6].stF(); sv.stF()
    for s in sc[1:]+[sv]: s.sent()
    oc.wait()

def k2_call(sv,cot,tok,D,FF,H,NZ,S):
    (qkv,pt,attT,hid,n1T,n2T,actT,slp,gq,go,gu,gd,vec)=sv
    R=n1T.shape[1]; nseq=R//S
    sds=jax.ShapeDtypeStruct; V=pltpu.VMEM; dma=pltpu.SemaphoreType.DMA
    rr=D//(8*NZ); rd=FF//(8*NZ); nd=8*NZ
    ins=(actT,cot.reshape(R,D),gd.reshape(FF,D),slp,n2T,gu.reshape(D,FF),hid,attT,go.reshape(D,D),qkv,pt,gq.reshape(D,3*D),n1T,tok.reshape(R,D),vec)
    outs=[sds((R,D),F32),sds((rr,3*D),F32),sds((rr,D),F32),sds((rr,FF),F32),sds((rd,D),F32)]+[sds((1,rr),F32)]*8+[sds((1,rd),F32)]
    vm=pl.BlockSpec(memory_space=pltpu.VMEM); anyb=pl.BlockSpec(memory_space=pl.ANY)
    pieces=[(rr,FF//2),(rr,FF//2),(rr,FF//2),(rr,FF//2),(rr,D),(rr,2*D),(rr,D)]
    scr=[V((FF,R),BF),V((R,D),BF),V((FF,D),BF),V((R,FF),BF),V((D,R),BF),V((D,FF),BF),V((R,D),F32),V((D,R),BF),V((D,D),BF),V((16,D),F32),
        V((2,2,S,S),BF),V((R,D),F32),V((R,D),BF),V((R,D),BF),V((R,3*D),BF),V((16,D),F32),V((1,FF),F32)]
    scr+=[V((2,NZ,4)+p,BF) for p in pieces[:2]]
    scr+=[V((NZ,4)+p,BF) for p in pieces]+[V((2,NZ)+p,BF) for p in pieces]+[V((NZ,)+p,BF) for p in pieces]+[V((NZ,)+p,BF) for p in pieces]
    scr+=[V((2,NZ,4)+p,BF) for p in (pieces[2],pieces[3],pieces[4],pieces[6])]
    vp=(16,128)
    scr+=[V((2,NZ,4)+vp,F32),V((NZ,4)+vp,F32),V((2,NZ)+vp,F32),V((NZ,)+vp,F32),V((NZ,)+vp,F32)]
    scr+=[dma((8,2,4)),dma((8,2,NZ)),dma((17,)),dma((2,)),dma((1,))]
    o=pl.pallas_call(functools.partial(k2_body,D,FF,H,NZ,nseq,S),out_shape=outs,in_specs=[anyb]*15,
        out_specs=[anyb]+[vm]*(len(outs)-1),scratch_shapes=scr,name="backward_scatter",
        compiler_params=pltpu.CompilerParams(collective_id=1,has_side_effects=True,vmem_limit_bytes=67043328))(*ins)
    return o
def per_device(NZ,tokens,segments,first_gain,first_shift,qkv_weight,query_bias,value_bias,out_weight,out_bias,second_gain,second_shift,up_weight,up_bias,down_weight,down_bias,cotangent):
    D=tokens.shape[2]; FF=up_weight.shape[1]; S=tokens.shape[1]; H=HEADS
    slab=make_slab((first_gain,first_shift,query_bias,value_bias,out_bias,second_gain,second_shift,down_bias),up_bias)
    out,*sv=k1_call(tokens,segments,slab,qkv_weight,out_weight,up_weight,down_weight,D,FF,H,NZ)
    tg,oq,oo,ou,od,*v=k2_call(sv,cotangent,tokens,D,FF,H,NZ,S)
    v=[a.reshape(-1) for a in v]
    return (out.reshape(tokens.shape),tg.reshape(tokens.shape),v[0],v[1],oq,v[2],v[3],oo,v[4],v[5],v[6],ou,v[8],od,v[7])
def specs_of(start):
    pass
def solution(mesh):
    d=("fsdp","dp")
    ins=(P(d,None,None),P(d,None),P("fsdp"),P("fsdp"),P("fsdp",None),P("fsdp"),P("fsdp"),P("fsdp",None),P("fsdp"),P("fsdp"),P("fsdp"),P("fsdp",None),P("fsdp"),P("fsdp",None),P("fsdp"),P(d,None,None))
    outs=(P(d,None,None),P(d,None,None),P(d),P(d),P(d,None),P(d),P(d),P(d,None),P(d),P(d),P(d),P(d,None),P(d),P(d,None),P(d))
    def run(*args):
        D,FF=args[11].shape; n=mesh.shape['fsdp']
        local=args[0].shape[0]//mesh.size
        whole=n%4==0 and mesh.shape['dp']==2 and D%(16*n)==0 and FF==4*D and local*args[0].shape[1]==D and D==64*HEADS and args[0].shape[1]%128==0
        body=functools.partial(per_device,n//4) if whole else per_device_plain
        return jax.shard_map(body,mesh=mesh,in_specs=ins,out_specs=outs,check_vma=False)(*args)
    return run
```

```python
import functools
import math

import jax
import jax.numpy as jnp
from jax import lax
from jax.experimental import pallas as pl
from jax.experimental.pallas import tpu as pltpu
from jax.sharding import PartitionSpec as P

HEADS = 12


EPSILON = 1e-06
SLOPE = math.sqrt(2.0 / math.pi)
CUBIC = 0.044715


def product(left_side, right_side):
    return jnp.dot(left_side, right_side, preferred_element_type=jnp.float32)


def product_left_turned(left_side, right_side):
    return lax.dot_general(
        left_side, right_side, (((0,), (0,)), ((), ())), preferred_element_type=jnp.float32
    )


def product_right_turned(left_side, right_side):
    return lax.dot_general(
        left_side, right_side, (((1,), (1,)), ((), ())), preferred_element_type=jnp.float32
    )


def norm_forward(features, norm_gain, norm_shift):
    centered = features - jnp.mean(features, axis=-1, keepdims=True)
    inv_spread = lax.rsqrt(jnp.mean(centered * centered, axis=-1, keepdims=True) + EPSILON)
    unit_rows = centered * inv_spread
    return (unit_rows * norm_gain + norm_shift, unit_rows, inv_spread)


def norm_backward(grad_normed, unit_rows, inv_spread, norm_gain):
    scaled = grad_normed * norm_gain
    inner = (
        scaled
        - jnp.mean(scaled, axis=-1, keepdims=True)
        - unit_rows * jnp.mean(scaled * unit_rows, axis=-1, keepdims=True)
    )
    return (
        inner * inv_spread,
        jnp.sum(grad_normed * unit_rows, axis=0),
        jnp.sum(grad_normed, axis=0),
    )


def smooth_gate(features):
    return (
        0.5
        * features
        * (1.0 + jnp.tanh(SLOPE * (features + CUBIC * features * features * features)))
    )


def gate_slope(features):
    bent = jnp.tanh(SLOPE * (features + CUBIC * features * features * features))
    return 0.5 * (1.0 + bent) + 0.5 * features * (1.0 - bent * bent) * SLOPE * (
        1.0 + 3.0 * CUBIC * features * features
    )


def masked_scores(queries, key_rows, same_image, score_scale):
    scores = (
        jnp.einsum("qhd,khd->hqk", queries, key_rows, preferred_element_type=jnp.float32)
        * score_scale
    )
    return jnp.where(same_image[None], scores, -1e30)


def attend_forward(queries, key_rows, values, same_image, score_scale):
    step_heads = queries.shape[1] // 4
    outputs = []
    totals = []
    for head_block in range(4):
        head_span = slice(head_block * step_heads, (head_block + 1) * step_heads)
        scores = masked_scores(
            queries[:, head_span], key_rows[:, head_span], same_image, score_scale
        )
        row_top = jnp.max(scores, axis=-1, keepdims=True)
        exponent = jnp.exp(scores - row_top)
        row_total = jnp.sum(exponent, axis=-1, keepdims=True)
        weights_low = (exponent / row_total).astype(jnp.bfloat16)
        outputs.append(
            jnp.einsum(
                "hqk,khd->qhd",
                weights_low,
                values[:, head_span],
                preferred_element_type=jnp.float32,
            )
        )
        totals.append(row_top + jnp.log(row_total))
    return (jnp.concatenate(outputs, axis=1), totals)


def attend_backward(queries, key_rows, values, same_image, score_scale, totals, grad_attended):
    step_heads = queries.shape[1] // 4
    query_parts = []
    key_parts = []
    value_parts = []
    for head_block in range(4):
        head_span = slice(head_block * step_heads, (head_block + 1) * step_heads)
        scores = masked_scores(
            queries[:, head_span], key_rows[:, head_span], same_image, score_scale
        )
        probability = jnp.exp(scores - totals[head_block])
        grad_piece = grad_attended[:, head_span]
        grad_values = jnp.einsum(
            "hqk,qhd->khd",
            probability.astype(jnp.bfloat16),
            grad_piece,
            preferred_element_type=jnp.float32,
        )
        grad_probs = jnp.einsum(
            "qhd,khd->hqk", grad_piece, values[:, head_span], preferred_element_type=jnp.float32
        )
        grad_scores = (
            probability * (grad_probs - jnp.sum(grad_probs * probability, axis=-1, keepdims=True))
        ).astype(jnp.bfloat16)
        grad_queries = (
            jnp.einsum(
                "hqk,khd->qhd",
                grad_scores,
                key_rows[:, head_span],
                preferred_element_type=jnp.float32,
            )
            * score_scale
        )
        grad_keys = (
            jnp.einsum(
                "hqk,qhd->khd",
                grad_scores,
                queries[:, head_span],
                preferred_element_type=jnp.float32,
            )
            * score_scale
        )
        query_parts.append(grad_queries.astype(jnp.bfloat16))
        key_parts.append(grad_keys.astype(jnp.bfloat16))
        value_parts.append(grad_values.astype(jnp.bfloat16))
    return (
        jnp.concatenate(query_parts, axis=1),
        jnp.concatenate(key_parts, axis=1),
        jnp.concatenate(value_parts, axis=1),
    )


def per_device_plain(
    tokens,
    segments,
    first_gain,
    first_shift,
    qkv_weight,
    query_bias,
    value_bias,
    out_weight,
    out_bias,
    second_gain,
    second_shift,
    up_weight,
    up_bias,
    down_weight,
    down_bias,
    cotangent,
):
    head_count = HEADS
    model_width = tokens.shape[2]
    head_width = model_width // head_count
    score_scale = 1.0 / math.sqrt(head_width)
    gain_one, shift_one, qkv_full, query_shift, value_shift, out_full, out_shift = (
        lax.all_gather(first_gain, "fsdp", axis=0, tiled=True),
        lax.all_gather(first_shift, "fsdp", axis=0, tiled=True),
        lax.all_gather(qkv_weight, "fsdp", axis=0, tiled=True),
        lax.all_gather(query_bias, "fsdp", axis=0, tiled=True),
        lax.all_gather(value_bias, "fsdp", axis=0, tiled=True),
        lax.all_gather(out_weight, "fsdp", axis=0, tiled=True),
        lax.all_gather(out_bias, "fsdp", axis=0, tiled=True),
    )
    gain_two, shift_two, up_full, up_shift, down_full, down_shift = (
        lax.all_gather(second_gain, "fsdp", axis=0, tiled=True),
        lax.all_gather(second_shift, "fsdp", axis=0, tiled=True),
        lax.all_gather(up_weight, "fsdp", axis=0, tiled=True),
        lax.all_gather(up_bias, "fsdp", axis=0, tiled=True),
        lax.all_gather(down_weight, "fsdp", axis=0, tiled=True),
        lax.all_gather(down_bias, "fsdp", axis=0, tiled=True),
    )
    first_scale = gain_one.astype(jnp.float32)
    first_offset = shift_one.astype(jnp.float32)
    second_scale = gain_two.astype(jnp.float32)
    second_offset = shift_two.astype(jnp.float32)
    query_offset = query_shift.astype(jnp.float32)
    value_offset = value_shift.astype(jnp.float32)
    out_offset = out_shift.astype(jnp.float32)
    up_offset = up_shift.astype(jnp.float32)
    down_offset = down_shift.astype(jnp.float32)
    micro_count = tokens.shape[0]
    saved = []
    outputs_low = []
    for batch_index in range(micro_count):
        inputs = tokens[batch_index].astype(jnp.float32)
        segment_row = segments[batch_index]
        same_image = segment_row[:, None] == segment_row[None, :]
        normed, unit_one, spread_one = norm_forward(inputs, first_scale, first_offset)
        normed_low = normed.astype(jnp.bfloat16)
        mixed_qkv = product(normed_low, qkv_full)
        queries = (
            (mixed_qkv[:, :model_width] + query_offset)
            .astype(jnp.bfloat16)
            .reshape(-1, head_count, head_width)
        )
        key_rows = (
            mixed_qkv[:, model_width : 2 * model_width]
            .astype(jnp.bfloat16)
            .reshape(-1, head_count, head_width)
        )
        values = (
            (mixed_qkv[:, 2 * model_width :] + value_offset)
            .astype(jnp.bfloat16)
            .reshape(-1, head_count, head_width)
        )
        attended, totals = attend_forward(queries, key_rows, values, same_image, score_scale)
        attended_low = attended.reshape(-1, model_width).astype(jnp.bfloat16)
        hidden = inputs + (product(attended_low, out_full) + out_offset)
        normed_two, unit_two, spread_two = norm_forward(hidden, second_scale, second_offset)
        normed_two_low = normed_two.astype(jnp.bfloat16)
        upward = product(normed_two_low, up_full) + up_offset
        active_low = smooth_gate(upward).astype(jnp.bfloat16)
        result = hidden + (product(active_low, down_full) + down_offset)
        outputs_low.append(result.astype(jnp.bfloat16))
        saved.append(
            (
                same_image,
                unit_one,
                spread_one,
                normed_low,
                queries,
                key_rows,
                values,
                totals,
                attended_low,
                unit_two,
                spread_two,
                normed_two_low,
                upward,
                active_low,
            )
        )
    gain_two_back, up_back, down_back = (
        lax.all_gather(second_gain, "fsdp", axis=0, tiled=True),
        lax.all_gather(up_weight, "fsdp", axis=0, tiled=True),
        lax.all_gather(down_weight, "fsdp", axis=0, tiled=True),
    )
    gain_one_back, qkv_back, out_back = (
        lax.all_gather(first_gain, "fsdp", axis=0, tiled=True),
        lax.all_gather(qkv_weight, "fsdp", axis=0, tiled=True),
        lax.all_gather(out_weight, "fsdp", axis=0, tiled=True),
    )
    first_scale_back = gain_one_back.astype(jnp.float32)
    second_scale_back = gain_two_back.astype(jnp.float32)
    accum = [
        jnp.zeros(item_array.shape, jnp.float32)
        for item_array in (
            gain_one,
            shift_one,
            qkv_full,
            query_shift,
            value_shift,
            out_full,
            out_shift,
            gain_two,
            shift_two,
            up_full,
            up_shift,
            down_full,
            down_shift,
        )
    ]
    grads_back = []
    for batch_index in range(micro_count):
        (
            same_image,
            unit_one,
            spread_one,
            normed_low,
            queries,
            key_rows,
            values,
            totals,
            attended_low,
            unit_two,
            spread_two,
            normed_two_low,
            upward,
            active_low,
        ) = saved[batch_index]
        grad_down = cotangent[batch_index]
        grad_top = grad_down.astype(jnp.float32)
        down_term = product_left_turned(active_low, grad_down)
        grad_active = product_right_turned(grad_down, down_back)
        grad_up = (grad_active * gate_slope(upward)).astype(jnp.bfloat16)
        up_term = product_left_turned(normed_two_low, grad_up)
        grad_normed_two = product_right_turned(grad_up, up_back)
        hidden_part, gain_two_term, shift_two_term = norm_backward(
            grad_normed_two, unit_two, spread_two, second_scale_back
        )
        grad_hidden = grad_top + hidden_part
        grad_branch = grad_hidden.astype(jnp.bfloat16)
        out_term = product_left_turned(attended_low, grad_branch)
        grad_attended = (
            product_right_turned(grad_branch, out_back)
            .astype(jnp.bfloat16)
            .reshape(-1, head_count, head_width)
        )
        grad_queries, grad_keys, grad_values = attend_backward(
            queries, key_rows, values, same_image, score_scale, totals, grad_attended
        )
        grad_queries = grad_queries.reshape(-1, model_width)
        grad_keys = grad_keys.reshape(-1, model_width)
        grad_values = grad_values.reshape(-1, model_width)
        grad_mixed = jnp.concatenate([grad_queries, grad_keys, grad_values], axis=1)
        qkv_term = product_left_turned(normed_low, grad_mixed)
        grad_normed = product_right_turned(grad_mixed, qkv_back)
        input_part, gain_one_term, shift_one_term = norm_backward(
            grad_normed, unit_one, spread_one, first_scale_back
        )
        grads_back.append(grad_hidden + input_part)
        terms = (
            gain_one_term,
            shift_one_term,
            qkv_term,
            jnp.sum(grad_queries.astype(jnp.float32), axis=0),
            jnp.sum(grad_values.astype(jnp.float32), axis=0),
            out_term,
            jnp.sum(grad_branch.astype(jnp.float32), axis=0),
            gain_two_term,
            shift_two_term,
            up_term,
            jnp.sum(grad_up.astype(jnp.float32), axis=0),
            down_term,
            jnp.sum(grad_top, axis=0),
        )
        accum = [earlier + later for earlier, later in zip(accum, terms)]
    shares = (
        lax.psum_scatter(accum[0], ("fsdp", "dp"), scatter_dimension=0, tiled=True),
        lax.psum_scatter(accum[1], ("fsdp", "dp"), scatter_dimension=0, tiled=True),
        lax.psum_scatter(accum[2], ("fsdp", "dp"), scatter_dimension=0, tiled=True),
        lax.psum_scatter(accum[3], ("fsdp", "dp"), scatter_dimension=0, tiled=True),
        lax.psum_scatter(accum[4], ("fsdp", "dp"), scatter_dimension=0, tiled=True),
        lax.psum_scatter(accum[5], ("fsdp", "dp"), scatter_dimension=0, tiled=True),
        lax.psum_scatter(accum[6], ("fsdp", "dp"), scatter_dimension=0, tiled=True),
        lax.psum_scatter(accum[7], ("fsdp", "dp"), scatter_dimension=0, tiled=True),
        lax.psum_scatter(accum[8], ("fsdp", "dp"), scatter_dimension=0, tiled=True),
        lax.psum_scatter(accum[9], ("fsdp", "dp"), scatter_dimension=0, tiled=True),
        lax.psum_scatter(accum[10], ("fsdp", "dp"), scatter_dimension=0, tiled=True),
        lax.psum_scatter(accum[11], ("fsdp", "dp"), scatter_dimension=0, tiled=True),
        lax.psum_scatter(accum[12], ("fsdp", "dp"), scatter_dimension=0, tiled=True),
    )
    return (
        jnp.stack(outputs_low),
        jnp.stack(grads_back),
        shares[0],
        shares[1],
        shares[2],
        shares[3],
        shares[4],
        shares[5],
        shares[6],
        shares[7],
        shares[8],
        shares[9],
        shares[10],
        shares[11],
        shares[12],
    )


MESH = pl.DeviceIdType.MESH

class Place:
    def __init__(s, nz):
        s.nz = nz
        s.f = lax.axis_index("fsdp"); s.c = lax.axis_index("dp")
        s.z = s.f // 4
        s.p = s.f % 4
        x = s.f % 2; y = (s.f // 2) % 2
        a = jnp.where(s.c == 0, x, y); b = jnp.where(s.c == 0, y, x)
        sa = jnp.where(s.c == 0, 1, 2); sb = jnp.where(s.c == 0, 2, 1)
        s.pa = s.p + (1 - 2 * a) * sa
        s.pb = s.p + (1 - 2 * b) * sb
        s.pab = s.pa + (1 - 2 * b) * sb
    def at(s, z, p, c=None):
        return {"fsdp": z * 4 + p, "dp": s.c if c is None else c}

def barrier(pc):
    bar = pltpu.get_barrier_semaphore()
    def sig(z, p, c=None):
        pl.semaphore_signal(bar, inc=1, device_id=pc.at(z, p, c), device_id_type=MESH)
    sig(pc.z, pc.pa); sig(pc.z, pc.pb); sig(pc.z, pc.p, 1 - pc.c)
    for d in range(1, pc.nz):
        @pl.when(pc.z >= d)
        def _(): sig(pc.z - d, pc.p)
        @pl.when(pc.z + d < pc.nz)
        def _(): sig(pc.z + d, pc.p)
    pl.semaphore_wait(bar, 3 + pc.nz - 1)

def others(pc, fn):
    for d in range(1, pc.nz):
        @pl.when(pc.z + d < pc.nz)
        def _(): fn(pc.z + d)
        @pl.when(pc.z >= d)
        def _(): fn(pc.z - d)

class Gather:
    def __init__(s, pc, k, kind, view, src, zs, ls, ss, so):
        s.pc, s.k, s.kind, s.view, s.src = pc, k, kind, view, src
        s.zs, s.ls, s.ss, s.so = zs, ls, ss, so
    def rc(s, src, dst, ssem, rsem, dev):
        return pltpu.make_async_remote_copy(src_ref=src, dst_ref=dst, send_sem=ssem, recv_sem=rsem, device_id=dev, device_id_type=MESH)
    def zc(s, z2, zo=None):
        pc = s.pc; v = s.view(pc.z if zo is None else zo, pc.p, pc.c)
        return s.rc(s.src, v, s.ss.at[s.k, z2], s.zs.at[s.k, pc.z if zo is None else zo], pc.at(z2, pc.p))
    def line(s, p, sem, dev, q):
        pc = s.pc; v = s.view(None, p, pc.c)
        return s.rc(v, v, s.so.at[s.k, q], s.ls.at[s.k, sem], dev)
    def a1(s): return s.line(s.pc.p, 0, s.pc.at(s.pc.z, s.pc.pa), 0)
    def b1(s): return s.line(s.pc.p, 1, s.pc.at(s.pc.z, s.pc.pb), 1)
    def b2(s): return s.line(s.pc.pa, 2, s.pc.at(s.pc.z, s.pc.pb), 2)
    def core(s, q):
        pc = s.pc
        return s.line((pc.p, pc.pa, pc.pb, pc.pab)[q], 3 + q, pc.at(pc.z, pc.p, 1 - pc.c), 3 + q)
    def st0(s):
        others(s.pc, lambda z2: s.zc(z2).start())
    def st1(s):
        pc = s.pc
        others(pc, lambda z2: s.zc(z2, zo=z2).wait_recv())
        s.a1().start(); s.b1().start(); s.core(0).start()
    def st2(s):
        s.a1().wait_recv()
        s.b2().start(); s.core(1).start()
    def st3(s):
        s.b1().wait_recv(); s.core(2).start()
    def st4(s):
        s.b2().wait_recv(); s.core(3).start()
    def fin(s):
        for q in range(4): s.core(q).wait_recv()
    def sent(s):
        others(s.pc, lambda z2: s.zc(z2).wait_send())
        s.a1().wait_send(); s.b1().wait_send(); s.b2().wait_send()
        for q in range(4): s.core(q).wait_send()

class GatherMinor(Gather):
    def piece(s, p, sem, dev, q, src=None):
        pc = s.pc; v = s.view(pc.z, p, pc.c)
        return s.rc(v if src is None else src, v, s.so.at[s.k, q], s.ls.at[s.k, sem], dev)
    def a1(s): return s.piece(s.pc.p, 0, s.pc.at(s.pc.z, s.pc.pa), 0, s.src)
    def b1(s): return s.piece(s.pc.p, 1, s.pc.at(s.pc.z, s.pc.pb), 1, s.src)
    def b2(s): return s.piece(s.pc.pa, 2, s.pc.at(s.pc.z, s.pc.pb), 2)
    def zc(s, z2, zo=None):
        pc = s.pc; v = s.view(pc.z if zo is None else zo, None, pc.c)
        return s.rc(v, v, s.ss.at[s.k, z2], s.zs.at[s.k, pc.z if zo is None else zo], pc.at(z2, pc.p))
    def corez(s, z):
        pc = s.pc; v = s.view(z, None, pc.c)
        return s.rc(v, v, s.so.at[s.k, 3 + z], s.ls.at[s.k, 3 + z], pc.at(pc.z, pc.p, 1 - pc.c))
    def st0(s):
        s.a1().start(); s.b1().start()
    def st1(s):
        s.a1().wait_recv(); s.b2().start()
    def st2(s):
        s.b1().wait_recv(); s.b2().wait_recv()
        others(s.pc, lambda z2: s.zc(z2).start())
        s.corez(s.pc.z).start()
    def st3(s):
        pass
    def st4(s):
        def go(z2):
            s.zc(z2, zo=z2).wait_recv(); s.corez(z2).start()
        others(s.pc, go)
    def fin(s):
        for z in range(s.pc.nz): s.corez(z).wait_recv()
    def sent(s):
        others(s.pc, lambda z2: s.zc(z2).wait_send())
        s.a1().wait_send(); s.b1().wait_send(); s.b2().wait_send()
        for z in range(s.pc.nz): s.corez(z).wait_send()
BF=jnp.bfloat16; F32=jnp.float32
EPS=EPSILON

class GatherVec(Gather):
    def a1(s): return s.line(s.pc.p, 0, s.pc.at(s.pc.z, s.pc.pa), 0)
    def st1(s):
        pc = s.pc
        others(pc, lambda z2: s.zc(z2, zo=z2).wait_recv())
        s.a1().start(); s.b1().start()
    def st2(s):
        s.a1().wait_recv(); s.b2().start()
    def fin(s): s.b1().wait_recv(); s.b2().wait_recv()
    def sent(s):
        others(s.pc, lambda z2: s.zc(z2).wait_send())
        s.a1().wait_send(); s.b1().wait_send(); s.b2().wait_send()

class GatherMinorR(GatherMinor):
    def up(s, zo):
        pc=s.pc; v=s.view(zo,None,pc.c)
        return s.rc(v,v,s.ss.at[s.k,zo],s.zs.at[s.k,zo],pc.at(pc.z+1,pc.p))
    def dn(s, zo):
        pc=s.pc; v=s.view(zo,None,pc.c)
        return s.rc(v,v,s.so.at[s.k,7+zo],s.zs.at[s.k,zo],pc.at(pc.z-1,pc.p))
    def st2(s):
        pc=s.pc
        s.b1().wait_recv(); s.b2().wait_recv()
        @pl.when(pc.z<pc.nz-1)
        def _(): s.up(pc.z).start()
        @pl.when(pc.z>0)
        def _(): s.dn(pc.z).start()
        s.corez(pc.z).start()
    def relay(s,d):
        pc=s.pc
        @pl.when(pc.z>=d)
        def _():
            s.up(pc.z-d).wait_recv()
            @pl.when(pc.z<pc.nz-1)
            def _(): s.up(pc.z-d).start()
            s.corez(pc.z-d).start()
        @pl.when(pc.z+d<pc.nz)
        def _():
            s.up(pc.z+d).wait_recv()
            @pl.when(pc.z>0)
            def _(): s.dn(pc.z+d).start()
            s.corez(pc.z+d).start()
    def st3(s): s.relay(1)
    def st4(s): s.relay(2)
    def st5(s):
        for d in range(3,s.pc.nz): s.relay(d)
    def sent(s):
        pc=s.pc
        for d in range(pc.nz):
            @pl.when((pc.z>=d)&(pc.z<pc.nz-1))
            def _(): s.up(pc.z-d).wait_send()
            @pl.when((pc.z+d<pc.nz)&(pc.z>0))
            def _(): s.dn(pc.z+d).wait_send()
        s.a1().wait_send(); s.b1().wait_send(); s.b2().wait_send()
        for z in range(s.pc.nz): s.corez(z).wait_send()

def dotT(a,b): return lax.dot_general(a,b,(((1,),(1,)),((),())),preferred_element_type=F32)
def dot(a,b): return jnp.dot(a,b,preferred_element_type=F32)
def dotL(a,b): return lax.dot_general(a,b,(((0,),(0,)),((),())),preferred_element_type=F32)

def loop(n, body, events=()):
    ev={}
    for i,fn in events: ev.setdefault(min(i,n-1),[]).append(fn)
    def step(i,_):
        body(i)
        for j in sorted(ev):
            @pl.when(i==j)
            def _():
                for fn in ev[j]: fn()
        return 0
    lax.fori_loop(0,n,step,0)

def norm(x, g, b):
    mean=jnp.mean(x,axis=-1,keepdims=True)
    cen=x-mean
    inv=lax.rsqrt(jnp.mean(cen*cen,axis=-1,keepdims=True)+EPS)
    return (cen*inv)*g+b

PLAN_F={
    'start':('V0', 'Q0', 'o0', 'd10', 'w0', 'u00', 'V1', 'd11', 'V2', 'u10', 'Vf', 'Q1', 'w1'),
    'vec':('Q2', 'Q3'),
    'n1':((1,('w2', 'd12', 'o1', 'w3', 'd00', 'Q4', 'u01')),(2,('Qf', 'w4', 'o2')),),
    'qk':((0,('o3', 'wf')),),
    'v':((0,('u11',)),),
    'at':((0,('d13',)),(1,('u02', 'o4')),(4,('u12', 'u03')),(5,('of', 'd01')),),
    'n2':((2,('u04',)),(5,('d14', 'u0f', 'u13')),),
    'ul':((0,('u14', 'd02', 'u1f')),(1,('d15', 'd03')),),
    'uh':((0,('d1f', 'd04')),(1,('d0f',)),),
    'mask':(),
}

def chunks(D, FF, down_rows):
    h=down_rows//2
    return [(0,0,None,0,D,'M'),(0,0,None,2*D,D//2,'M'),(1,0,None,0,D//2,'M'),(2,0,None,0,FF//4,'M'),(2,0,None,FF//2,FF//4,'M'),(3,0,h,0,D//2,'M'),(3,h,h,0,D//2,'N')]

def k1_body(D,FF,H,NZ,nseq,S,ev_lag, *refs):
    (tok,segr,*refs)=refs
    vin=refs[:9]
    (wq,wo,wu,wd,
     out_h,qkv_h,pt_h,att_h,hid_h,n1_h,n2_h,act_h,slp_h,gq_h,go_h,gu_h,gd_h,vec_h,
     gq,go,gu,gd,vbuf,n1,qkv,att,hid,n2,act,slp,outb,pst,bias,vec,upb,n1t,n2t,attt,actt,
     slab,zs,lsem,ss,so,loc,hsem,psem)=refs[9:]
    R=nseq*S
    pc=Place(NZ)
    bufs=[gq,go,gu,gd]; ws=[wq,wo,wu,wd]
    CH=chunks(D,FF,wd.shape[0])
    gs=[]; own=[]
    for k,(wi,r0,nr,c0,ncol,kind) in enumerate(CH):
        nr=ws[wi].shape[0] if nr is None else nr
        def view(z,p,c,wi=wi,r0=r0,nr=nr,c0=c0,ncol=ncol):
            zi=slice(None) if z is None else z
            pi=slice(None) if p is None else p
            return bufs[wi].at[zi,pi,pl.ds(r0,nr),pl.ds(pl.multiple_of(c*ncol+c0,128),ncol)]
        src=ws[wi].at[pl.ds(r0,nr),pl.ds(pl.multiple_of(pc.c*ncol+c0,128),ncol)]
        gs.append((Gather if kind=='M' else GatherMinorR)(pc,k,kind,view,src,zs,lsem,ss,so))
        cp=pltpu.make_async_copy(src, view(pc.z,pc.p,pc.c), loc.at[k]); cp.start(); own.append(cp)
    def vview(z,p,c):
        return vbuf.at[slice(None) if z is None else z, slice(None) if p is None else p]
    slab[...]=jnp.zeros_like(slab)
    for q in range(8): slab[q:q+1,:D//(4*NZ)]=vin[q][...].astype(F32)
    slab[8:9,:]=vin[8][:,:128].astype(F32); slab[9:10,:FF//(4*NZ)-128]=vin[8][:,128:].astype(F32)
    kv=len(CH)
    gv=GatherVec(pc,kv,'V',vview,slab,zs,lsem,ss,so)
    cp=pltpu.make_async_copy(slab, vview(pc.z,pc.p,pc.c), loc.at[kv]); cp.start(); own.append(cp)
    barrier(pc)
    ev={}
    for nm,g in zip(('Q','w','o','u0','u1','d0','d1','V'),gs+[gv]):
        for st in '012345': ev[nm+st]=getattr(g,'st'+st,None)
        ev[nm+'f']=g.fin
    run=lambda name,n,body: loop(n,body,[(i,ev[e]) for i,es in PLAN_F.get(name,()) for e in es])
    for cp in own: cp.wait()
    for e in PLAN_F['start']: ev[e]()
    sends=[]
    def put(src,dst,sem):
        c=pltpu.make_async_copy(src,dst,sem); c.start(); sends.append(c)
    for q in range(nseq):
        row=jnp.broadcast_to(segr[q:q+1,:],(S,S))
        bias[q]=jnp.where(row==row.T,0.0,-1e30).astype(F32)
    for e in PLAN_F['mask']: ev[e]()
    rows=[vbuf[i//4,i%4] for i in range(4*NZ)]
    nv=D//(4*NZ)
    vec[...]=jnp.concatenate([r[:,:nv] for r in rows],axis=1)
    upb[...]=jnp.concatenate([jnp.concatenate([r[8:9,:],r[9:10,:FF//(4*NZ)-128]],axis=1) for r in rows],axis=1)
    for e in PLAN_F['vec']: ev[e]()
    BR=128
    def n1b(i):
        r=pl.ds(pl.multiple_of(i*BR,BR),BR)
        y=norm(tok[r,:].astype(F32),vec[0:1,:],vec[1:2,:]).astype(BF)
        n1[r,:]=y
        n1t[:,r]=y.T
    run('n1',R//BR,n1b)
    put(n1t,n1_h,hsem.at[0]); put(vec,vec_h,hsem.at[1])
    TN=256
    def qk(j):
        y=dot(n1[...],gq[:,:,:,pl.ds(pl.multiple_of(j*D,128),D)].reshape(D,D))
        b=jnp.where(j==0,vec[2:3,:],jnp.where(j==1,0.0,vec[3:4,:]))
        qkv[pl.ds(pl.multiple_of(j*R,128),R),:]=(y+b).astype(BF)
    run('qk',2,qk)
    run('v',1,lambda j: qk(2))
    put(qkv,qkv_h,hsem.at[3])
    put(gq,gq_h,hsem.at[4])
    HP=H//2
    lane=lax.broadcasted_iota(jnp.int32,(1,128),1)
    def attn(i,sl):
        s=i//HP; hp=i%HP
        r=pl.ds(pl.multiple_of(s*S,128),S)
        hc=pl.ds(pl.multiple_of(hp*128,128),128)
        q2,k2,v2=[qkv[pl.ds(pl.multiple_of(w*R+s*S,128),S),hc] for w in range(3)]
        vT=v2.T
        @pl.when(i>=2)
        def _(): pltpu.make_async_copy(pst.at[sl],pt_h.at[i-2],psem.at[sl]).wait()
        q=q2*BF(0.125)
        km=jnp.concatenate([jnp.where(lane<64,k2,BF(0)),jnp.where(lane<64,BF(0),k2)],axis=0)
        for x in range(0,S,128):
            sc=dotT(km,q[x:x+128])
            for h in range(2):
                sT=sc[h*S:(h+1)*S]+bias[s,:,x:x+128]
                m=jnp.max(sT,axis=0,keepdims=True)
                e=jnp.exp(sT-m)
                l=jnp.sum(e,axis=0,keepdims=True)
                pst[sl,h,:,x:x+128]=(e*(1.0/l)).astype(BF)
        oT=jnp.concatenate([dot(vT[64*h:64*h+64],pst[sl,h]) for h in range(2)],axis=0).astype(BF)
        attt[hc,r]=oT
        att[r,hc]=oT.T
        pltpu.make_async_copy(pst.at[sl],pt_h.at[i],psem.at[sl]).start()
    def attn2(i):
        for sl in range(2): attn(2*i+sl,sl)
    run('at',nseq*HP//2,attn2)
    put(attt,att_h,hsem.at[5])
    put(go,go_h,hsem.at[6])
    def op(j):
        hid[...]=dot(att[...],go[...].reshape(D,D))+vec[4:5,:]+tok[...].astype(F32)
    run('op',1,op)
    put(hid,hid_h,hsem.at[7])
    def n2b(i):
        r=pl.ds(pl.multiple_of(i*BR,BR),BR)
        y=norm(hid[r,:],vec[5:6,:],vec[6:7,:]).astype(BF)
        n2[r,:]=y
        n2t[:,r]=y.T
    run('n2',R//BR,n2b)
    put(n2t,n2_h,hsem.at[8])
    def upj(j):
        c=pl.ds(pl.multiple_of(j*D,128),D)
        w=gu[:,:,:,c].reshape(D,D)
        u=dot(n2[...],w)+upb[:,c]
        u2=u*u
        t=jnp.tanh(SLOPE*(u+CUBIC*u*u2))
        hp1=0.5*(1.0+t)
        a=(u*hp1).astype(BF)
        act[:,c]=a
        actt[c,:]=a.T
        slp[:,c]=(hp1+0.5*u*(1.0-t*t)*(SLOPE*(1.0+3.0*CUBIC*u2))).astype(BF)
    run('ul',FF//2//D,upj)
    run('uh',FF//2//D,lambda j: upj(j+FF//2//D))
    put(gu,gu_h,hsem.at[9])
    put(actt,act_h,hsem.at[10]); put(slp,slp_h,hsem.at[11])
    put(gd,gd_h,hsem.at[12])
    def dn(j):
        c=pl.ds(pl.multiple_of(j*TN,TN),TN)
        w=gd[:,:,:,c].reshape(FF,TN)
        outb[:,c]=(dot(act[...],w)+vec[7:8,c]+hid[:,c]).astype(BF)
    run('dn',D//TN,dn)
    put(outb,out_h,hsem.at[13])
    n=nseq*HP
    for i in (n-2,n-1):
        pltpu.make_async_copy(pst.at[i%2],pt_h.at[i],psem.at[i%2]).wait()
    for g in gs: g.sent()
    gv.sent()
    for c in sends: c.wait()

def k1_call(tok,segr,vs,wq,wo,wu,wd,D,FF,H,NZ):
    nseq,S=tok.shape[0],tok.shape[1]
    R=nseq*S
    sds=jax.ShapeDtypeStruct
    g4=[(NZ,4)+w.shape for w in (wq,wo,wu,wd)]
    outs=[sds((R,D),BF),sds((3*R,D),BF),sds((nseq*H//2,2,S,S),BF),sds((D,R),BF),sds((R,D),F32),sds((D,R),BF),sds((D,R),BF),sds((FF,R),BF),sds((R,FF),BF)]+[sds(g,BF) for g in g4]+[sds((16,D),F32)]
    V=pltpu.VMEM
    n=8
    scr=[V(g,BF) for g in g4]+[V((NZ,4,16,128),F32),V((R,D),BF),V((3*R,D),BF),V((R,D),BF),V((R,D),F32),V((R,D),BF),V((R,FF),BF),V((R,FF),BF),V((R,D),BF),V((2,2,S,S),BF),V((nseq,S,S),F32),V((16,D),F32),V((1,FF),F32),V((D,R),BF),V((D,R),BF),V((D,R),BF),V((FF,R),BF)]
    dma=pltpu.SemaphoreType.DMA
    scr+=[V((16,128),F32)]
    scr+=[dma((n,NZ)),dma((n,7)),dma((n,NZ)),dma((n,7+NZ)),dma((n,)),dma((14,)),dma((2,))]
    vm=pl.BlockSpec(memory_space=pltpu.VMEM); anyb=pl.BlockSpec(memory_space=pl.ANY)
    flops=2*R*D*(4*D+2*FF)
    return pl.pallas_call(functools.partial(k1_body,D,FF,H,NZ,nseq,S,1),
        out_shape=outs,in_specs=[vm]*15,out_specs=[anyb]*len(outs),scratch_shapes=scr,name="gather_forward",
        compiler_params=pltpu.CompilerParams(collective_id=0,has_side_effects=True,vmem_limit_bytes=63*1024*1024))(
        tok.reshape(R,D),segr,*[v[None] for v in vs],wq,wo,wu,wd)


PLAN_B={
    'l1':((7,('d0P',)),),
    'l2':((0,('d1P', 'd0B')),(3,('d0A',)),),
    'u0':((1,('d1B', 'u0P')),),
    'u1':((1,('u1P',)),),
    'l4':((1,('u1B',)),(2,('d1A',)),),
    'l5':((5,('d0Z',)),),
    'ow':((0,('u1A',)),),
    'at0_':((0,('u0B',)),(1,('d1Z', 'oP')),),
    'at1_':((0,('a0P', 'u1Z', 'a0B', 'u0A', 'oB')),),
    'at2_':((0,('a1P', 'a0A')),),
    'qw2_':((0,('a1B', 'u1F', 'u0Z')),),
    'l9':((0,('oA', 'a2P')),(1,('a1A', 'a2B', 'a0Z')),),
    'l10':((1,('oZ',)),),
    'end':('u0F', 'vP', 'a2A', 'a1Z', 'vB', 'vA', 'a2Z', 'oF', 'd0F', 'd1F', 'vZ', 'a1F', 'a2F', 'a0F', 'vF'),
}

class Scatter:
    def __init__(s, pc, k, g, pb_, bb, ab, zb, out, sem, zsem, kv):
        s.pc,s.k,s.g,s.pb_,s.bb,s.ab,s.zb,s.out,s.sem,s.zsem=pc,k,g,pb_,bb,ab,zb,out,sem,zsem
    def rc(s,src,dst,q,dev):
        return pltpu.make_async_remote_copy(src_ref=src,dst_ref=dst,send_sem=s.sem.at[s.k,0,q],recv_sem=s.sem.at[s.k,1,q],device_id=dev,device_id_type=MESH)
    def pair(s):
        pc=s.pc
        return s.rc(s.g.at[1-pc.c], s.pb_, 0, pc.at(pc.z,pc.p,1-pc.c))
    def b(s,w):
        pc=s.pc
        return s.rc(s.g.at[pc.c,:,(pc.pb,pc.pab)[w]], s.bb.at[w], 1+w, pc.at(pc.z,pc.pb))
    def a(s):
        pc=s.pc
        return s.rc(s.g.at[pc.c,:,pc.pa], s.ab, 3, pc.at(pc.z,pc.pa))
    def zc(s,z2):
        pc=s.pc
        return pltpu.make_async_remote_copy(src_ref=s.g.at[pc.c,z2,pc.p],dst_ref=s.zb.at[pc.z],send_sem=s.zsem.at[s.k,0,z2],recv_sem=s.zsem.at[s.k,1,pc.z],device_id=pc.at(z2,pc.p),device_id_type=MESH)
    def zr(s,zo):
        pc=s.pc
        return pltpu.make_async_remote_copy(src_ref=s.g.at[pc.c,zo,pc.p],dst_ref=s.zb.at[zo],send_sem=s.zsem.at[s.k,0,zo],recv_sem=s.zsem.at[s.k,1,zo],device_id=pc.at(zo,pc.p),device_id_type=MESH)
    def stP(s): s.pair().start()
    def stB(s):
        pc=s.pc; s.pair().wait_recv()
        for w,p in enumerate((pc.pb,pc.pab)):
            def add(z,_,p=p):
                s.g[pc.c,z,p]=s.g[pc.c,z,p]+s.pb_[z,p]
                return 0
            lax.fori_loop(0,pc.nz,add,0)
        s.b(1).start(); s.b(0).start()
    def stA(s):
        pc=s.pc; s.b(1).wait_recv()
        def add(z,_):
            s.g[pc.c,z,pc.pa]=(s.g[pc.c,z,pc.pa].astype(F32)+s.pb_[z,pc.pa].astype(F32)+s.bb[1,z].astype(F32)).astype(s.g.dtype)
            return 0
        lax.fori_loop(0,pc.nz,add,0)
        s.a().start()
    def stZ(s):
        pc=s.pc; s.b(0).wait_recv(); s.a().wait_recv()
        def add(z,_):
            s.g[pc.c,z,pc.p]=(s.g[pc.c,z,pc.p].astype(F32)+s.pb_[z,pc.p].astype(F32)+(s.bb[0,z].astype(F32)+s.ab[z].astype(F32))).astype(s.g.dtype)
            return 0
        lax.fori_loop(0,pc.nz,add,0)
        s.zb[pc.z]=s.g[pc.c,pc.z,pc.p]
        others(pc, lambda z2: s.zc(z2).start())
    def stF(s):
        pc=s.pc
        others(pc, lambda z2: s.zr(z2).wait_recv())
        t=s.zb[0].astype(F32)
        for z in range(1,pc.nz): t=t+s.zb[z].astype(F32)
        s.out(t)
    def sent(s):
        s.pair().wait_send(); s.b(0).wait_send(); s.b(1).wait_send(); s.a().wait_send()
        others(s.pc, lambda z2: s.zc(z2).wait_send())

def k2_body(D,FF,H,NZ,nseq,S,*refs):
    (actT_h,cot_h,gd_h,slp_h,n2T_h,gu_h,hid_h,attT_h,go_h,qkv_h,pt_h,gq_h,n1T_h,tok_h,vec_h,
     tg_h,o_q,o_o,o_u,o_d,*rest)=refs
    o_v=rest[0]
    (actT,cot,gd,slp,n2T,gu,hid,attT,go,vec,pst,dn,br,datt,dqkv,vg,ug,
     gd0,gd1,*rest)=rest[1:]
    ps,bs,as_,zs,rest=rest[:8],rest[8:16],rest[16:24],rest[24:32],rest[32:]
    (gu0,gu1,gout,gv,vgb,vp,vb,va,vz,dsb,sem,zsem,lsem,psem,osem)=rest
    R=nseq*S
    pc=Place(NZ)
    qkv,n1T,gq,tok,gqk=actT.at[pl.ds(0,3*R)],actT.at[pl.ds(3*R,R)],gd,n2T,gd0
    names=[actT,cot,gd,slp,n2T,gu,hid,attT,go,qkv,None,n1T,tok,vec]
    srcs=[actT_h,cot_h,gd_h,slp_h,n2T_h,gu_h,hid_h,attT_h,go_h,qkv_h,None,n1T_h,tok_h,vec_h]
    ld={}
    def fetch(*ks):
        for i in ks:
            ld[i]=pltpu.make_async_copy(srcs[i],names[i],lsem.at[i]); ld[i].start()
    need=lambda *ks: [ld[k].wait() for k in ks]
    gqc=[pltpu.make_async_copy(gq_h.at[:,pl.ds(w*D,D)],gq.at[pl.ds(w*D,D)],lsem.at[14+w]) for w in range(3)]
    fetch(0,1,2,3,4,5,6,13,7,8)
    barrier(pc)
    rr=D//(8*NZ); rd=FF//(8*NZ)
    def outd(r0):
        def fn(t):
            for w in range(2): o_d[pl.ds(r0+w*rr,rr),:]=t[:,w*D:(w+1)*D]
        return fn
    def outw(ref,r0,c0):
        def fn(t):
            ref[pl.ds(r0,t.shape[0]),pl.ds(c0,t.shape[1])]=t
        return fn
    HF=FF//2
    def outa(n):
        def fn(t):
            for w in range(3): o_q[:,w*D+n*TN:w*D+(n+1)*TN]=t[:,w*TN:(w+1)*TN]
        return fn
    TN=256
    ng=D//TN
    half=lambda w: gd0.at[:,:,:,:,pl.ds(w*D,D)]
    ga=[half(0),half(1),gv]
    names8=('d0','d1','u0','u1','o','a0','a1','a2')
    gs8=(gd0,gd1,gu0,gu1,gout,*ga)
    fo=(outd(0),outd(rd//2),outw(o_u,0,0),outw(o_u,0,HF),outw(o_o,0,0),outa(0),outa(1),outa(2))
    sc={nm:Scatter(pc,i,gs8[i],ps[i],bs[i],as_[i],zs[i],fo[i],sem,zsem,0) for i,nm in enumerate(names8)}
    ev={}
    for nm in names8:
        for st in 'PBAZF': ev[nm+st]=getattr(sc[nm],'st'+st)
    run=lambda name,n,body: loop(n,body,[(i,ev[e]) for i,es in PLAN_B.get(name,()) for e in es])
    lanes=lambda j,w=TN: pl.ds(pl.multiple_of(j*w,128),w)
    vg[...]=jnp.zeros_like(vg)
    need(0,1)
    def l1(i):
        y=dot(actT[pl.ds(pl.multiple_of(i*4*rd,128),4*rd),:],cot[...]).astype(BF)
        for d in range(2):
            for c in range(2):
                for h,g in enumerate((gd0,gd1)):
                    o=(d*2+c)*rd+h*(rd//2)
                    for w in range(2): g[c,i//2,2*(i%2)+d,:,w*D:(w+1)*D]=y[o+w*rr:o+(w+1)*rr]
    run('l1',2*NZ,l1)
    fetch(9,11)
    need(2,3)
    def l2(j):
        c=lanes(j,D)
        da=dotT(cot[...],gd[pl.ds(pl.multiple_of(j*D,128),D),:])
        du=(da*slp[:,c].astype(F32)).astype(BF)
        slp[:,c]=du
        ug[:,c]=jnp.sum(du.astype(F32),axis=0,keepdims=True)
    run('l2',FF//D,l2)
    for c in gqc: c.start()
    need(4)
    def scat(g,lhs,rhs,rhs_c,g_c):
        w=g_c.size
        y=dot(lhs[...],rhs[:,rhs_c]).reshape(NZ,4,2,rr,w)
        for c in range(2):
            for z in range(NZ):
                g[c,z,:,:,g_c]=y[z,:,c].astype(BF)
    nh=HF//D
    run('u0',nh,lambda j: scat(gu0,n2T,slp,lanes(j,D),lanes(j,D)))
    run('u1',nh,lambda j: scat(gu1,n2T,slp,lanes(j+nh,D),lanes(j,D)))
    fetch(12)
    need(5)
    def l4(j):
        dn[:,lanes(j)]=dotT(slp[...],gu[pl.ds(pl.multiple_of(j*TN,TN),TN),:])
    run('l4',D//TN,l4)
    need(6,13)
    BR=128
    def back(x,g,gain,top):
        mean=jnp.mean(x,axis=-1,keepdims=True)
        cen=x-mean
        inv=lax.rsqrt(jnp.mean(cen*cen,axis=-1,keepdims=True)+EPS)
        unit=cen*inv
        sg=g*gain
        inner=sg-jnp.mean(sg,axis=-1,keepdims=True)-unit*jnp.mean(sg*unit,axis=-1,keepdims=True)
        return top+inner*inv, jnp.sum(g*unit,axis=0,keepdims=True), jnp.sum(g,axis=0,keepdims=True)
    def l5(i):
        r=pl.ds(pl.multiple_of(i*BR,BR),BR)
        ct=cot[r,:].astype(F32)
        h,gg,gs=back(hid[r,:],dn[r,:],vec[5:6,:],ct)
        hid[r,:]=h
        hb=h.astype(BF)
        br[r,:]=hb
        vg[5:6,:]+=gg; vg[6:7,:]+=gs
        vg[4:5,:]+=jnp.sum(hb.astype(F32),axis=0,keepdims=True)
        vg[7:8,:]+=jnp.sum(ct,axis=0,keepdims=True)
    run('l5',R//BR,l5)
    need(7,8)
    run('ow',1,lambda j: scat(gout,attT,br,lanes(0,D),lanes(0,D)))
    def l6(j):
        datt[...]=dotT(br[...],go[...]).astype(BF)
    run('l6',1,l6)
    need(9)
    HP=H//2
    n=nseq*HP
    lane=lax.broadcasted_iota(jnp.int32,(1,128),1)
    pcopy=lambda i,sl: pltpu.make_async_copy(pt_h.at[(i%nseq)*HP+i//nseq],pst.at[sl],psem.at[sl])
    pcopy(0,0).start(); pcopy(1,1).start()
    def l7(i,sl):
        s=i%nseq; hp=i//nseq
        r=pl.ds(pl.multiple_of(s*S,128),S)
        c0,c1,c2=[pl.ds(pl.multiple_of(w*D+hp*128,128),128) for w in range(3)]
        pcopy(i,sl).wait()
        q2,k2,v2=[actT[pl.ds(pl.multiple_of(w*R+s*S,128),S),c0] for w in range(3)]; da=datt[r,c0]
        kT=k2.T
        vm=jnp.concatenate([jnp.where(lane<64,v2,BF(0)),jnp.where(lane<64,BF(0),v2)],axis=0)
        for x in range(0,S,128):
            dp=dotT(vm,da[x:x+128])
            for h in range(2):
                pf=pst[sl,h,:,x:x+128].astype(F32)
                t=dp[h*S:(h+1)*S]*pf
                dsb[h,:,x:x+128]=(t-pf*jnp.sum(t,axis=0,keepdims=True)).astype(BF)
        dvb=dot(pst[sl].reshape(2*S,S),da)
        dkb=dot(dsb[...].reshape(2*S,S),q2)
        dvv=jnp.where(lane<64,dvb[:S],dvb[S:]).astype(BF)
        dkk=(jnp.where(lane<64,dkb[:S],dkb[S:])*0.125).astype(BF)
        dq=[dot(kT[64*h:64*h+64],dsb[h]) for h in range(2)]
        dqq=(jnp.concatenate(dq,axis=0).T*0.125).astype(BF)
        dqkv[r,c0]=dqq; dqkv[r,c1]=dkk; dqkv[r,c2]=dvv
        vg[2:3,c0]+=jnp.sum(dqq.astype(F32),axis=0,keepdims=True)
        vg[3:4,c0]+=jnp.sum(dvv.astype(F32),axis=0,keepdims=True)
        @pl.when(i+2<n)
        def _(): pcopy(i+2,sl).start()
    def l7b(i):
        for sl in range(2): l7(2*i+sl,sl)
    need(11)
    per=n//ng//2
    for g in range(ng):
        run('at%d_'%g,per,lambda i,g=g: l7b(i+g*per))
        if g==0: sc['d0'].sent()
        def qw(i,g=g):
            for w in range(3): scat(ga[g],n1T,dqkv,pl.ds(w*D+g*TN,TN),pl.ds(w*TN,TN))
        run('qw%d_'%g,1,qw)
    for c in gqc: c.wait()
    need(12)
    def l9(j):
        dn[:,lanes(j)]=sum(dotT(dqkv[:,w*D:(w+1)*D],gq[pl.ds(pl.multiple_of(w*D+j*TN,TN),TN),:]) for w in range(3))
    run('l9',D//TN,l9)
    def l10(i):
        r=pl.ds(pl.multiple_of(i*BR,BR),BR)
        t,gg,gs=back(tok[r,:].astype(F32),dn[r,:],vec[0:1,:],hid[r,:])
        dn[r,:]=t
        vg[0:1,:]+=gg; vg[1:2,:]+=gs
    run('l10',R//BR,l10)
    oc=pltpu.make_async_copy(dn,tg_h,osem.at[0]); oc.start()
    nv=D//(4*NZ); nu=FF//(4*NZ)
    for i in range(4*NZ):
        for c in range(2):
            vgb[c,i//4,i%4]=jnp.concatenate([jnp.pad(vg[0:8,nv*i+c*(nv//2):nv*i+(c+1)*(nv//2)],((0,0),(0,128-nv//2))),
               jnp.pad(ug[:,nu*i+c*(nu//2):nu*i+(c+1)*(nu//2)],((0,7),(0,128-nu//2)))],axis=0)
    def outv(t): o_v[...]=t
    sv=Scatter(pc,8,vgb,vp,vb,va,vz,outv,sem,zsem,0)
    for st in 'PBAZF': ev['v'+st]=getattr(sv,'st'+st)
    for e in PLAN_B['end']: ev[e]()
    for nm in names8[1:]: sc[nm].sent()
    sv.sent()
    oc.wait()

def k2_call(sv,cot,tok,D,FF,H,NZ,S):
    (qkv,pt,attT,hid,n1T,n2T,actT,slp,gq,go,gu,gd,vec)=sv
    R=n1T.shape[1]; nseq=R//S
    sds=jax.ShapeDtypeStruct; V=pltpu.VMEM; dma=pltpu.SemaphoreType.DMA
    rr=D//(8*NZ); rd=FF//(8*NZ); nd=8*NZ
    ins=(actT,cot.reshape(R,D),gd.reshape(FF,D),slp,n2T,gu.reshape(D,FF),hid,attT,go.reshape(D,D),qkv,pt,gq.reshape(D,3*D),n1T,tok.reshape(R,D),vec)
    outs=[sds((R,D),F32),sds((rr,3*D),F32),sds((rr,D),F32),sds((rr,FF),F32),sds((rd,D),F32)]+[sds((16,128),F32)]
    vm=pl.BlockSpec(memory_space=pltpu.VMEM); anyb=pl.BlockSpec(memory_space=pl.ANY)
    pieces=[(rr,FF//2),(rr,FF//2),(rr,FF//2),(rr,FF//2),(rr,D),(rr,D),(rr,D),(rr,D)]
    scr=[V((FF,R),BF),V((R,D),BF),V((FF,D),BF),V((R,FF),BF),V((D,R),BF),V((D,FF),BF),V((R,D),F32),V((D,R),BF),V((D,D),BF),V((16,D),F32),
        V((2,2,S,S),BF),V((R,D),F32),V((R,D),BF),V((R,D),BF),V((R,3*D),BF),V((16,D),F32),V((1,FF),F32)]
    scr+=[V((2,NZ,4)+p,BF) for p in pieces[:2]]
    scr+=[V((NZ,4)+p,BF) for p in pieces]+[V((2,NZ)+p,BF) for p in pieces]+[V((NZ,)+p,BF) for p in pieces]+[V((NZ,)+p,BF) for p in pieces]
    scr+=[V((2,NZ,4)+p,BF) for p in (pieces[2],pieces[3],pieces[4],pieces[7])]
    vp=(16,128)
    scr+=[V((2,NZ,4)+vp,F32),V((NZ,4)+vp,F32),V((2,NZ)+vp,F32),V((NZ,)+vp,F32),V((NZ,)+vp,F32)]
    scr+=[V((2,S,S),BF)]
    scr+=[dma((9,2,4)),dma((9,2,NZ)),dma((17,)),dma((2,)),dma((1,))]
    o=pl.pallas_call(functools.partial(k2_body,D,FF,H,NZ,nseq,S),out_shape=outs,in_specs=[anyb]*15,
        out_specs=[anyb]+[vm]*(len(outs)-1),scratch_shapes=scr,name="backward_scatter",
        compiler_params=pltpu.CompilerParams(collective_id=1,has_side_effects=True,vmem_limit_bytes=67043328))(*ins)
    return o

def finish_body(D,FF,n,*refs):
    k=2*n
    ins=refs[:n]; small=refs[n]; outs=refs[n+1:k+1]; vecs=refs[k+1:k+10]; bufs=refs[k+10:k+10+n]; si,so=refs[k+10+n:]
    cut=lambda i: [(o,ins[i].shape[0]//4) for o in range(0,ins[i].shape[0],ins[i].shape[0]//4)] if ins[i].shape[0]%64==0 else [(0,ins[i].shape[0])]
    jobs=[]
    for i in range(n):
        for j,(o,w) in enumerate(cut(i)):
            r=pl.ds(o,w)
            a=pltpu.make_async_copy(ins[i].at[r],bufs[i].at[r],si.at[i,j])
            a.start(); jobs.append((a,pltpu.make_async_copy(bufs[i].at[r],outs[i].at[r],so.at[i,j])))
    t=small[...]
    for q in range(9): vecs[q][...]=t[q:q+1,:vecs[q].shape[1]]
    for a,b in jobs: a.wait(); b.start()
    for a,b in jobs: b.wait()

def finish_call(large,small,D,FF,nv,nu):
    sds=jax.ShapeDtypeStruct; V=pltpu.VMEM; dma=pltpu.SemaphoreType.DMA
    n=len(large)
    vm=pl.BlockSpec(memory_space=pltpu.VMEM); anyb=pl.BlockSpec(memory_space=pl.ANY)
    return pl.pallas_call(functools.partial(finish_body,D,FF,n),
        out_shape=[sds(a.shape,a.dtype) for a in large]+[sds((1,nv),F32)]*8+[sds((1,nu),F32)],
        in_specs=[anyb]*n+[vm],out_specs=[anyb]*n+[vm]*9,
        scratch_shapes=[V(a.shape,a.dtype) for a in large]+[dma((n,4)),dma((n,4))],name="hand_out",
        compiler_params=pltpu.CompilerParams(vmem_limit_bytes=67043328))(*large,small)
def per_device(NZ,tokens,segments,first_gain,first_shift,qkv_weight,query_bias,value_bias,out_weight,out_bias,second_gain,second_shift,up_weight,up_bias,down_weight,down_bias,cotangent):
    D=tokens.shape[2]; FF=up_weight.shape[1]; S=tokens.shape[1]; H=HEADS
    vs=(first_gain,first_shift,query_bias,value_bias,out_bias,second_gain,second_shift,down_bias,up_bias)
    out,*sv=k1_call(tokens,segments,vs,qkv_weight,out_weight,up_weight,down_weight,D,FF,H,NZ)
    tg,oq,oo,ou,od,small=k2_call(sv,cotangent,tokens,D,FF,H,NZ,S)
    out,tg,oq,oo,ou,od,*v=finish_call((out,tg,oq,oo,ou,od),small,D,FF,D//(8*NZ),FF//(8*NZ))
    v=[a.reshape(-1) for a in v]
    return (out.reshape(tokens.shape),tg.reshape(tokens.shape),v[0],v[1],oq,v[2],v[3],oo,v[4],v[5],v[6],ou,v[8],od,v[7])
def specs_of(start):
    pass
def solution(mesh):
    d=("fsdp","dp")
    ins=(P(d,None,None),P(d,None),P("fsdp"),P("fsdp"),P("fsdp",None),P("fsdp"),P("fsdp"),P("fsdp",None),P("fsdp"),P("fsdp"),P("fsdp"),P("fsdp",None),P("fsdp"),P("fsdp",None),P("fsdp"),P(d,None,None))
    outs=(P(d,None,None),P(d,None,None),P(d),P(d),P(d,None),P(d),P(d),P(d,None),P(d),P(d),P(d),P(d,None),P(d),P(d,None),P(d))
    def run(*args):
        D,FF=args[11].shape; n=mesh.shape['fsdp']
        local=args[0].shape[0]//mesh.size
        whole=n%4==0 and mesh.shape['dp']==2 and D%(16*n)==0 and FF==4*D and local*args[0].shape[1]==D and D==64*HEADS and args[0].shape[1]%128==0
        body=functools.partial(per_device,n//4) if whole else per_device_plain
        return jax.shard_map(body,mesh=mesh,in_specs=ins,out_specs=outs,check_vma=False)(*args)
    return run
```
